128 devices in a mesh: pipe: 4 (over x), expert: 32 (over z, y, core).
Axes of the slice: x: 4, y: 4, z: 4, core: 2. Of those that a mesh axis runs over, the one named last changes fastest.
Arguments:
- grad_rows: bfloat16 [2, 4, 4096, 3584], P(None, 'pipe', 'expert'), may hold values from -0.29882812 to 0.29882812
- expert_ids: int32 [2, 4, 4096, 8], P(None, 'pipe', 'expert'), may hold values from 0 to 31, all different within a row; in each aligned block of 128 rows (0 to 127, 128 to 255, ..., all dimensions but the last counted through in order) at most 40 rows name the same one
- gate_buckets: int32 [2, 4, 4096, 8], P(None, 'pipe', 'expert'), may hold values from 1 to 64
- saved_hidden: bfloat16 [2, 4, 32, 1280, 1280], P(None, 'pipe', 'expert'), may hold values from -6 to 6
Outputs:
- weight_grad: bfloat16 [4, 32, 1280, 3584], P('pipe', 'expert')
The draws below stay inside these ranges and needn't reach their ends.
Inputs may be any that keep to these rules, and one draw needn't show every extreme that they name: `expert_ids`: in every direction and rank, each aligned block of 128 tokens names each expert in at most 40 routes and some expert in exactly 40; the 8 ids of a token differ.
All inputs are finite; a program needn't handle non-finite values.
Results may differ from the reference program's by a relative error of at most 0.0058.
Values may be sent and summed in bfloat16 or wider, within the bound.
A program may use at most 128 MiB of HBM per device.

```python
import math
import jax
import jax.numpy as jnp
import numpy as np
from jax import lax

D = 3584
F = 1280
TOPK = 8
TOK_DEV = 128
EXPERTS = 32
TOKENS = 4096
CAP = 40
SLOTS = 1280
N_PIPE = 4
N_EXPERT = 32


def with_ends(drawn, key, least, largest):
    dims = drawn.shape
    spot = [jax.random.randint(jax.random.fold_in(key, axis), (), 0, dims[axis]) for axis in range(len(dims))]
    drawn = drawn.at[tuple(spot)].set(least)
    longest = dims.index(max(dims))
    spot[longest] = (spot[longest] + 1) % dims[longest]
    return drawn.at[tuple(spot)].set(largest)


def shard_levels(own_key, shape, cuts, smallest, top_value):
    loudness = 1.0
    for dim, blocks in cuts:
        heights = jax.random.uniform(jax.random.fold_in(jax.random.fold_in(own_key, 6), dim), (blocks,), jnp.float32, smallest / len(cuts), top_value / len(cuts))
        loudness = loudness * jnp.repeat(jnp.exp(heights), shape[dim] // blocks).reshape((-1,) + (1,) * (len(shape) - 1 - dim))
    return loudness


def assign_block(rng, own, number, rows, count, top, most, skew):
    ranking = jax.random.permutation(rng, count)
    packed, common = load_shares(count, rows * top, most, skew, True), load_shares(count, rows * top, most, skew, False)
    places = jnp.arange(count)

    def named(lengths, offset_by):
        used = int((lengths > 0).sum())
        fixed = max(1, used // 4)
        shifted = fixed + (places - fixed + offset_by * (used - fixed)) % max(1, count - fixed)
        return jnp.zeros((count,), jnp.int32).at[ranking[jnp.where(places < fixed, places, shifted)]].set(jnp.asarray(lengths, jnp.int32))

    lengths = jnp.where(number % 4 == 0, named(packed, number // 4), named(common, number - number // 4 - 1))
    mixed = jax.random.permutation(jax.random.fold_in(own, 3), count)
    donor, sink = mixed[0:count // 2 * 2:2], mixed[1:count // 2 * 2:2]
    margin = jnp.minimum(lengths[donor] - 1, most - lengths[sink]) // 2
    margin = jnp.where((donor == ranking[0]) | (sink == ranking[0]) | (lengths[sink] == 0), 0, jnp.maximum(margin, 0))
    shifted = jax.random.randint(jax.random.fold_in(own, 4), (count // 2,), 0, 1 << 20) % (margin + 1)
    lengths = lengths.at[donor].add(-shifted).at[sink].add(shifted)
    items = jnp.searchsorted(jnp.cumsum(lengths), jnp.arange(rows * top), side="right").astype(jnp.int32)
    grid = items.reshape(top, rows).T
    grid = grid[jax.random.permutation(jax.random.fold_in(own, 1), rows)]
    offset_by = jax.random.randint(jax.random.fold_in(own, 2), (rows, 1), 0, top)
    return jnp.take_along_axis(grid, (jnp.arange(top)[None, :] + offset_by) % top, axis=1)


def load_shares(number_of, total, reach, slope, full):
    loads = [(1 << 20) // math.isqrt(grade ** slope) + 1 for grade in range(1, number_of + 1)]
    largest = reach if full else min(reach, max(-(-total // number_of), total * loads[0] // sum(loads)))
    least = 1 if total - largest >= number_of - 1 else 0
    given, surplus = [largest] + [least] * (number_of - 1), total - largest - least * (number_of - 1)
    while surplus > 0:
        movable = [i for i in range(1, number_of) if given[i] < largest] or [i for i in range(1, number_of) if given[i] < reach]
        pool, left = sum([loads[i] for i in movable]), surplus
        for i in movable:
            extra = min(reach - given[i], max(1, left * loads[i] // pool), surplus)
            given[i] = given[i] + extra
            surplus = surplus - extra
    return np.array(given)


def noise(rng, dims, scale, reach, split=(), kind=jnp.bfloat16):
    drawn = jax.random.normal(rng, dims, jnp.float32) * scale
    if len(split) > 0:
        drawn = shard_levels(rng, dims, split, -0.22, 0.18) * drawn
    return jnp.clip(drawn, min=-reach, max=reach).astype(kind)


def setup_inputs(seed: int = 0) -> dict:
    keys = jax.random.split(jax.random.key(seed), 5)
    grad_rows = noise(keys[0], (2, N_PIPE, TOKENS, D), 0.05, 0.29882812, ((1, 4), (2, 32)))
    expert_ids_keys = jax.random.split(jax.random.fold_in(keys[1], 1), 2 * N_PIPE * TOKENS // TOK_DEV)
    expert_ids_turns = jax.random.permutation(jax.random.fold_in(keys[1], 3), 2 * N_PIPE * TOKENS // TOK_DEV)
    expert_ids = jax.vmap(lambda own, number: assign_block(jax.random.fold_in(keys[1], 2), own, number, TOK_DEV, EXPERTS, TOPK, CAP, 1))(expert_ids_keys, expert_ids_turns).reshape((2, N_PIPE, TOKENS, TOPK))
    gate_buckets = with_ends(jax.random.randint(keys[2], (2, N_PIPE, TOKENS, TOPK), 1, 65), jax.random.fold_in(keys[2], 1), 1, 64).astype(jnp.int32)
    saved_hidden = noise(keys[3], (2, N_PIPE, EXPERTS, SLOTS, F), 1.0, 6.0, ((1, 4), (2, 32)))
    return {"grad_rows": grad_rows, "expert_ids": expert_ids, "gate_buckets": gate_buckets, "saved_hidden": saved_hidden}


def build_outbound(token_rows, route_ids, bucket_ids):
    flat_ids = route_ids.reshape(-1)
    one_hot = (flat_ids[:, None] == jnp.arange(EXPERTS, dtype=jnp.int32)[None, :]).astype(jnp.int32)
    earlier = jnp.cumsum(one_hot, axis=0) - one_hot
    position = jnp.sum(earlier * one_hot, axis=1)
    slot_ids = flat_ids * CAP + position
    weighting = bucket_ids.reshape(-1).astype(jnp.float32) / 64.0
    slot_table = (slot_ids[:, None] == jnp.arange(EXPERTS * CAP, dtype=jnp.int32)[None, :]).astype(jnp.float32)
    slot_table = slot_table * weighting[:, None]
    spread = jnp.sum(slot_table.reshape(TOK_DEV, TOPK, EXPERTS * CAP), axis=1).astype(jnp.bfloat16)
    outbound = lax.dot_general(spread, token_rows, (((0,), (0,)), ((), ())), preferred_element_type=jnp.float32)
    return outbound.astype(jnp.bfloat16).reshape(EXPERTS, CAP, D)


def arrived_rows(token_rows, route_ids, bucket_ids):
    blocks = (token_rows.reshape(N_EXPERT, TOK_DEV, D), route_ids.reshape(N_EXPERT, TOK_DEV, TOPK), bucket_ids.reshape(N_EXPERT, TOK_DEV, TOPK))
    sent = lax.map(lambda pieces: build_outbound(pieces[0], pieces[1], pieces[2]), blocks)
    return jnp.moveaxis(sent, 1, 0).reshape(EXPERTS, SLOTS, D)


def per_expert(pieces):
    first_in, second_in, first_hidden, second_hidden = pieces
    first_part = jnp.dot(first_hidden.T, first_in, preferred_element_type=jnp.float32).astype(jnp.bfloat16)
    second_part = jnp.dot(second_hidden.T, second_in, preferred_element_type=jnp.float32).astype(jnp.bfloat16)
    return (first_part.astype(jnp.float32) + second_part.astype(jnp.float32)).astype(jnp.bfloat16)


def reference(grad_rows, expert_ids, gate_buckets, saved_hidden):
    section_grads = []
    for section in range(N_PIPE):
        mirror = N_PIPE - 1 - section
        first_in = arrived_rows(grad_rows[0, section], expert_ids[0, section], gate_buckets[0, section])
        second_in = arrived_rows(grad_rows[1, mirror], expert_ids[1, mirror], gate_buckets[1, mirror])
        section_grads.append(lax.map(per_expert, (first_in, second_in, saved_hidden[0, section], saved_hidden[1, mirror])))
    return jnp.stack(section_grads)
```

```python
import jax
import jax.numpy as jnp
from jax import lax
from jax.sharding import PartitionSpec as P


def build_outbound(token_rows, route_ids, bucket_ids, experts, capacity):
    tokens = token_rows.shape[0]
    member = route_ids[:, :, None] == jnp.arange(experts, dtype=jnp.int32)[None, None, :]
    named = jnp.any(member, axis=1)
    weight = jnp.sum(jnp.where(member, bucket_ids[:, :, None], 0), axis=1).astype(jnp.float32) / 64.0
    before = jnp.arange(tokens)[:, None] < jnp.arange(tokens)[None, :]
    rank = lax.dot_general(
        named.astype(jnp.bfloat16), before.astype(jnp.bfloat16), (((0,), (0,)), ((), ())),
        preferred_element_type=jnp.float32,
    )
    rank = jnp.where(named.T, rank, -1.0)
    slots = jnp.arange(capacity, dtype=jnp.float32)
    spread = jnp.where(rank[:, None, :] == slots[None, :, None], weight.T[:, None, :], 0.0)
    spread = spread.astype(jnp.bfloat16).reshape(experts * capacity, tokens)
    outbound = lax.dot_general(
        spread, token_rows, (((1,), (0,)), ((), ())), preferred_element_type=jnp.float32
    )
    return outbound.astype(jnp.bfloat16).reshape(experts, capacity, token_rows.shape[1])


def on_device(grad_rows, expert_ids, gate_buckets, saved_hidden):
    experts = lax.axis_size("expert")
    ranks = lax.axis_size("pipe")
    capacity = saved_hidden.shape[3] // experts
    mirror = [(i, ranks - 1 - i) for i in range(ranks)]

    def mirrored(value):
        return lax.ppermute(value, "pipe", mirror)

    rows = (grad_rows[0, 0], mirrored(grad_rows[1, 0]))
    ids = (expert_ids[0, 0], mirrored(expert_ids[1, 0]))
    buckets = (gate_buckets[0, 0], mirrored(gate_buckets[1, 0]))
    hidden = (saved_hidden[0, 0, 0], mirrored(saved_hidden[1, 0, 0]))
    parts = []
    for index in range(2):
        outbound = build_outbound(rows[index], ids[index], buckets[index], experts, capacity)
        arrived = lax.all_to_all(outbound, "expert", split_axis=0, concat_axis=0, tiled=True)
        parts.append(
            lax.dot_general(
                hidden[index], arrived.reshape(-1, arrived.shape[-1]), (((0,), (0,)), ((), ())),
                preferred_element_type=jnp.float32,
            ).astype(jnp.bfloat16)
        )
    total = parts[0].astype(jnp.float32) + parts[1].astype(jnp.float32)
    return total.astype(jnp.bfloat16)[None, None]


def solution(mesh):
    return jax.shard_map(
        on_device,
        mesh=mesh,
        in_specs=(
            P(None, "pipe", "expert", None),
            P(None, "pipe", "expert", None),
            P(None, "pipe", "expert", None),
            P(None, "pipe", "expert", None, None),
        ),
        out_specs=P("pipe", "expert", None, None),
        check_vma=False,
    )
```

```python
import functools

import jax
import jax.numpy as jnp
from jax import lax
from jax.experimental import pallas as pl
from jax.experimental.pallas import tpu as pltpu
from jax.sharding import PartitionSpec as P

MESH = pl.DeviceIdType.MESH
SIDE = 4
CORES = 2
LANES = 128
WIDE = 2 * LANES
TRACKS = 2
BF = jnp.bfloat16
F32 = jnp.float32


def wrap(i):
    return lax.rem(i + 2 * SIDE, SIDE)


def kernel(ranks, cap, tok_ref, ids_ref, gate_ref, hid_ref, out_ref,
           src, ring, pair, tiles, hid_t, hid_out, stage, select, own_tab, tab, tabs,
           to_far, to_sib, done,
           src_sem, x_sem, xt_sem, xh_sem, xsend_sem, stage_sem,
           ring_sem, own_sem, ring_send, pair_sem, pair_send,
           tab_sem, tab_own_sem, tab_send, tab_pair_sem, tab_pair_send,
           tile_sem, far_send, sib_send, done_sem):
    tokens, width = tok_ref.shape[1], tok_ref.shape[2]
    slots, units = hid_ref.shape[1], hid_ref.shape[2]
    half = width // CORES
    chunks = half // WIDE
    steps = 2 * chunks
    both = CORES * cap
    piece = units // SIDE

    rank = lax.axis_index("pipe")
    expert = lax.axis_index("expert")
    c = lax.rem(expert, CORES)
    y = lax.rem(expert // CORES, SIDE)
    z = expert // (CORES * SIDE)
    mine_a = (1 - c) * z + c * y
    mine_b = (1 - c) * y + c * z
    step_a = lax.rem(mine_b, 2)
    near = wrap(mine_b + 1 - 2 * step_a)
    far = wrap(mine_b - 1 + 2 * step_a)

    def at(z_, y_, core):
        return {"pipe": rank, "expert": (z_ * SIDE + y_) * CORES + core}

    def at_ab(a_, b_, core):
        return at((1 - c) * a_ + c * b_, (1 - c) * b_ + c * a_, core)

    def expert_ab(a_, b_, core):
        return (((1 - c) * a_ + c * b_) * SIDE + (1 - c) * b_ + c * a_) * CORES + core

    sibling = at(z, y, 1 - c)
    mirror = {"pipe": ranks - 1 - rank, "expert": expert}

    def send(s_ref, d_ref, s_sem, r_sem, dev):
        pltpu.make_async_remote_copy(
            src_ref=s_ref, dst_ref=d_ref, send_sem=s_sem, recv_sem=r_sem,
            device_id=dev, device_id_type=MESH).start()

    def await_bytes(ref, sem):
        pltpu.make_async_copy(ref, ref, sem).wait()

    first = pltpu.make_async_copy(tok_ref.at[0], src.at[0], src_sem)
    first.start()

    def load_hidden(n):
        d, part = (1, n) if n < slots // WIDE else (0, n - slots // WIDE)
        return pltpu.make_async_copy(
            hid_ref.at[d, pl.ds(part * WIDE, WIDE)], stage.at[n % 2], stage_sem.at[n % 2])

    load_hidden(0).start()
    load_hidden(1).start()

    barrier = pltpu.get_barrier_semaphore()
    friends = [sibling, mirror]
    for core in range(CORES):
        for turn in (1, SIDE - 1):
            friends.append(at(wrap(z + turn), y, core))
            friends.append(at(z, wrap(y + turn), core))
    for friend in friends:
        pl.semaphore_signal(barrier, inc=1, device_id=friend, device_id_type=MESH)
    pl.semaphore_wait(barrier, len(friends))

    for k in range(chunks):
        for h in range(CORES):
            cols = pl.ds(h * half + k * WIDE, WIDE)
            send(tok_ref.at[1, :, cols], src.at[1, :, cols], xsend_sem.at[0], x_sem.at[k], mirror)

    e_row = lax.broadcasted_iota(jnp.int32, (SIDE * SIDE * CORES, tokens), 0)
    before = (lax.broadcasted_iota(jnp.int32, (tokens, tokens), 0)
              < lax.broadcasted_iota(jnp.int32, (tokens, tokens), 1)).astype(F32).astype(BF)
    for d in range(2):
        ids = ids_ref[d]
        top = ids.shape[0]
        named = jnp.zeros(e_row.shape, F32)
        for j in range(top):
            named += jnp.where(e_row == ids[j:j + 1, :], 1.0, 0.0)
        earlier = jnp.dot(named.astype(BF), before, preferred_element_type=F32)
        spots = [jnp.sum(jnp.where(e_row == ids[j:j + 1, :], earlier, 0.0), axis=0, keepdims=True)
                 for j in range(top)]
        into = tab.at[0] if d == 0 else own_tab
        into[0] = ids.astype(F32)
        into[1] = jnp.concatenate(spots, axis=0)
        into[2] = gate_ref[d].astype(F32) / 64.0

    first.wait()

    def ring_out(source, dest, sems, send_sem, own, cols_of):
        for h in range(CORES):
            a_h = z if h == 0 else y
            for turn in (1, -1):
                dev = at(wrap(z + turn), y, 0) if h == 0 else at(z, wrap(y + turn), 1)
                which = 2 * c if turn == 1 else 2 - c
                send(cols_of(source, h), dest.at[a_h * CORES + c], send_sem, sems.at[which], dev)
        sib_a = c * z + (1 - c) * y
        send(cols_of(source, 1 - c), dest.at[sib_a * CORES + c], send_sem, sems.at[2], sibling)
        pltpu.make_async_copy(cols_of(source, c), dest.at[mine_a * CORES + c], own).start()

    def ring_on(dest, sems, send_sem):
        for turn, core in ((1, 0), (-1, 1)):
            part = dest.at[wrap(mine_a - turn) * CORES + core]
            await_bytes(part, sems.at[core])
            send(part, part, send_sem, sems.at[2], at_ab(wrap(mine_a + turn), mine_b, c))

    def step_cols(k):
        return lambda ref, h: ref.at[:, pl.ds(pl.multiple_of(h * half + k * WIDE, LANES), WIDE)]

    def stage_a(s):
        d, k = s // chunks, lax.rem(s, chunks)

        @pl.when(d == 1)
        def _():
            await_bytes(src.at[1, :, pl.ds(0, 2 * WIDE)], x_sem.at[k])

        @pl.when(k == 0)
        def _():
            @pl.when(d == 1)
            def _():
                await_bytes(tab.at[1], xt_sem)
            ring_out(tab.at[d], tabs.at[d, 0], tab_sem.at[d], tab_send.at[d], tab_own_sem.at[d],
                     lambda ref, h: ref)

        ring_out(src.at[d], ring.at[s], ring_sem.at[s], ring_send.at[s], own_sem.at[s], step_cols(k))

    def stage_b(s):
        d, k = s // chunks, lax.rem(s, chunks)

        @pl.when(k == 0)
        def _():
            ring_on(tabs.at[d, 0], tab_sem.at[d], tab_send.at[d])

        ring_on(ring.at[s], ring_sem.at[s], ring_send.at[s])

    def stage_c(s):
        d, k = s // chunks, lax.rem(s, chunks)

        @pl.when(k == 0)
        def _():
            await_bytes(tabs.at[d, 0, pl.ds(0, 5)], tab_sem.at[d, 2])
            await_bytes(tabs.at[d, 0, 0], tab_own_sem.at[d])
            for p, friend in ((0, near), (1, far)):
                send(tabs.at[d, 0], tabs.at[d, 1 + p], tab_pair_send.at[d], tab_pair_sem.at[d],
                     at_ab(mine_a, friend, c))

        await_bytes(ring.at[s, pl.ds(0, 5)], ring_sem.at[s, 2])
        await_bytes(ring.at[s, 0], own_sem.at[s])
        for p, friend in ((0, near), (1, far)):
            send(ring.at[s, :, :, pl.ds(p * LANES, LANES)], pair.at[s, p], pair_send.at[s],
                 pair_sem.at[s], at_ab(mine_a, friend, c))

    row = lax.broadcasted_iota(jnp.int32, (both, CORES * tokens), 0)
    lane = lax.broadcasted_iota(jnp.int32, (both, CORES * tokens), 1)
    target = jnp.where((row < cap) == (lane < tokens), jnp.where(row < cap, row, row - cap), -2).astype(F32)

    def select_rows(d, where_, a_, e):
        found = []
        for core in range(CORES):
            t = tabs.at[d, where_, a_ * CORES + core]
            hit = t[0] == e.astype(F32)
            spot = jnp.sum(jnp.where(hit, t[1] + 1.0, 0.0), axis=0, keepdims=True) - 1.0
            weight = jnp.sum(jnp.where(hit, t[2], 0.0), axis=0, keepdims=True)
            found.append((spot, weight))
        spot = jnp.concatenate([f[0] for f in found], axis=1)
        weight = jnp.concatenate([f[1] for f in found], axis=1)
        return jnp.where(spot == target, weight, 0.0).astype(BF)

    own2 = [(mine_b, c), (mine_b, 1 - c)]
    near2 = [(near, 0), (near, 1)]
    far2 = [(far, 0), (far, 1)]
    plan = [(0, x) for x in near2 + own2 + far2] + [(1, x) for x in own2 + far2] + [(2, x) for x in near2 + own2]

    def build_select(d):
        @pl.loop(0, SIDE)
        def _(a_):
            for n, (where_, (b_, core)) in enumerate(plan):
                select[a_, pl.ds(n * both, both), :] = select_rows(d, where_, a_, expert_ab(mine_a, b_, core))

    lead = {(0, 0): 2, (0, 1): 6, (1, 0): 0, (1, 1): 10}

    def stage_d(s):
        d, k = s // chunks, lax.rem(s, chunks)
        track = lax.rem(s, TRACKS)

        @pl.when(k == 0)
        def _():
            await_bytes(tabs.at[d, pl.ds(1, 2)], tab_pair_sem.at[d])
            build_select(d)

        @pl.when(s >= TRACKS)
        def _():
            await_bytes(to_far.at[track], far_send.at[track])
            await_bytes(to_sib.at[track], sib_send.at[track])

        await_bytes(ring.at[s], pair_sem.at[s])
        for p in range(2):
            friend = near if p == 0 else far
            for b_at in range(2):
                b_ = mine_b if b_at == 0 else friend
                start = lead[(p, b_at)] * both

                @pl.loop(0, SIDE)
                def _(a_):
                    if b_at == 0:
                        rows = ring[s, pl.ds(a_ * CORES, CORES), :, p * LANES:(p + 1) * LANES]
                    else:
                        rows = pair[s, p, pl.ds(a_ * CORES, CORES)]
                    rows = rows.reshape(CORES * tokens, LANES)
                    got = jnp.dot(select[a_, pl.ds(start, 4 * both), :], rows,
                                  preferred_element_type=F32).astype(BF)
                    own_at = 0 if p == 0 else 2 * both
                    far_at = 2 * both if p == 0 else 0
                    z_, y_ = (1 - c) * a_ + c * b_, (1 - c) * b_ + c * a_
                    tiles[1 + s * CORES + c, z_, y_, :, p * LANES:(p + 1) * LANES] = got[own_at:own_at + both]
                    to_sib[track, p, b_at, a_] = got[own_at + both:own_at + 2 * both]
                    for core in range(CORES):
                        to_far[track, p, core, b_at, a_] = got[far_at + core * both:far_at + (core + 1) * both]

        for h in range(CORES):
            @pl.when(c == h)
            def _():
                into = tiles.at[1 + s * CORES + h]
                for p in range(2):
                    cols = pl.ds(p * LANES, LANES)
                    friend = near if p == 0 else far
                    other = far if p == 0 else near
                    for b_at in range(2):
                        b_ = mine_b if b_at == 0 else friend
                        part = into.at[:, b_, :, cols] if h == 0 else into.at[b_, :, :, cols]
                        for core in range(CORES):
                            send(to_far.at[track, p, core, b_at], part, far_send.at[track],
                                 tile_sem.at[s * CORES + h], at_ab(mine_a, other, core))
                        send(to_sib.at[track, p, b_at], part, sib_send.at[track],
                             tile_sem.at[s * CORES + h], sibling)

    def stage_e(s):
        d, k = s // chunks, lax.rem(s, chunks)
        await_bytes(tiles.at[0, pl.ds(0, 2)], tile_sem.at[s * CORES + c])
        await_bytes(tiles.at[0], tile_sem.at[s * CORES + 1 - c])

        @pl.when(d == 0)
        def _():
            @pl.loop(0, CORES)
            def _(h):
                t = s * CORES + h

                @pl.loop(0, SIDE)
                def _(f):
                    got = jnp.dot(hid_t[0, pl.ds(f * piece, piece), :], tiles[t + 1].reshape(slots, WIDE),
                                  preferred_element_type=F32)
                    tiles[t, f] = got.astype(BF).reshape(SIDE, both, WIDE)

        @pl.when(s == chunks)
        def _():
            await_bytes(hid_t.at[1], xh_sem)

        @pl.when(d == 1)
        def _():
            @pl.loop(0, CORES)
            def _(h):
                t = s * CORES + h

                @pl.when(s > chunks)
                def _():
                    await_bytes(done.at[h], done_sem.at[h])

                @pl.loop(0, SIDE)
                def _(f):
                    got = jnp.dot(hid_t[1, pl.ds(f * piece, piece), :], tiles[t + 1].reshape(slots, WIDE),
                                  preferred_element_type=F32)
                    prior = tiles[t - chunks * CORES, f].reshape(piece, WIDE)
                    done[h, pl.ds(f * piece, piece), :] = (got + prior.astype(F32)).astype(BF)

                pltpu.make_async_copy(
                    done.at[h],
                    out_ref.at[:, pl.ds(pl.multiple_of(h * half + k * WIDE, LANES), WIDE)],
                    done_sem.at[h]).start()

    def transpose_hidden():
        parts = slots // WIDE
        for n in range(2 * parts):
            load_hidden(n).wait()
            into = hid_out if n < parts else hid_t.at[0]
            part = n % parts

            @pl.loop(0, units // WIDE)
            def _(f):
                at_f = pl.multiple_of(f * WIDE, WIDE)
                into[pl.ds(at_f, WIDE), part * WIDE:(part + 1) * WIDE] = stage[n % 2, :, pl.ds(at_f, WIDE)].T

            if n + 2 < 2 * parts:
                load_hidden(n + 2).start()

    stage_a(jnp.int32(0))
    send(own_tab, tab.at[1], xsend_sem.at[1], xt_sem, mirror)
    stage_a(jnp.int32(1))
    stage_b(jnp.int32(0))
    transpose_hidden()
    send(hid_out, hid_t.at[1], xsend_sem.at[2], xh_sem, mirror)

    def turn(i, carry):
        for lag, work in ((0, stage_a), (1, stage_b), (2, stage_c), (3, stage_d), (4, stage_e)):
            skip = {0: 2, 1: 1}.get(lag, 0)

            @pl.when((i - lag >= skip) & (i - lag < steps))
            def _():
                work(i - lag)
        return carry

    lax.fori_loop(2, steps + 4, turn, 0)

    for h in range(CORES):
        await_bytes(done.at[h], done_sem.at[h])
    for track in range(TRACKS):
        await_bytes(to_far.at[track], far_send.at[track])
        await_bytes(to_sib.at[track], sib_send.at[track])
    await_bytes(src.at[1], xsend_sem.at[0])
    await_bytes(own_tab, xsend_sem.at[1])
    await_bytes(hid_out, xsend_sem.at[2])

    @pl.loop(0, steps)
    def _(s):
        await_bytes(ring.at[s, pl.ds(0, 7)], ring_send.at[s])
        await_bytes(ring.at[s], pair_send.at[s])

    for d in range(2):
        await_bytes(tabs.at[d, 0, pl.ds(0, 7)], tab_send.at[d])
        await_bytes(tabs.at[d, pl.ds(1, 2)], tab_pair_send.at[d])


def on_device(ranks, grad_rows, expert_ids, gate_buckets, saved_hidden):
    tok, hid = grad_rows[:, 0], saved_hidden[:, 0, 0]
    ids = expert_ids[:, 0].transpose(0, 2, 1)
    gates = gate_buckets[:, 0].transpose(0, 2, 1)
    tokens, width = tok.shape[1:]
    top = ids.shape[1]
    slots, units = hid.shape[1:]
    cap = slots // (SIDE * SIDE * CORES)
    both = CORES * cap
    steps = width // WIDE
    dma = pltpu.SemaphoreType.DMA
    result = pl.pallas_call(
        functools.partial(kernel, ranks, cap),
        out_shape=jax.ShapeDtypeStruct((units, width), BF),
        in_specs=[
            pl.BlockSpec(memory_space=pl.ANY),
            pl.BlockSpec(memory_space=pltpu.VMEM),
            pl.BlockSpec(memory_space=pltpu.VMEM),
            pl.BlockSpec(memory_space=pl.ANY),
        ],
        out_specs=pl.BlockSpec(memory_space=pl.ANY),
        scratch_shapes=[
            pltpu.VMEM((2, tokens, width), BF),
            pltpu.VMEM((steps, SIDE * CORES, tokens, WIDE), BF),
            pltpu.VMEM((steps, 2, SIDE * CORES, tokens, LANES), BF),
            pltpu.VMEM((1 + steps * CORES, SIDE, SIDE, both, WIDE), BF),
            pltpu.VMEM((2, units, slots), BF),
            pltpu.VMEM((units, slots), BF),
            pltpu.VMEM((2, WIDE, units), BF),
            pltpu.VMEM((SIDE, 14 * both, CORES * tokens), BF),
            pltpu.VMEM((3, top, tokens), F32),
            pltpu.VMEM((2, 3, top, tokens), F32),
            pltpu.VMEM((2, 3, SIDE * CORES, 3, top, tokens), F32),
            pltpu.VMEM((TRACKS, 2, CORES, 2, SIDE, both, LANES), BF),
            pltpu.VMEM((TRACKS, 2, 2, SIDE, both, LANES), BF),
            pltpu.VMEM((CORES, units, WIDE), BF),
            dma, dma((steps // 2,)), dma, dma, dma((3,)), dma((2,)),
            dma((steps, 3)), dma((steps,)), dma((steps,)), dma((steps,)), dma((steps,)),
            dma((2, 3)), dma((2,)), dma((2,)), dma((2,)), dma((2,)),
            dma((steps * CORES,)), dma((TRACKS,)), dma((TRACKS,)), dma((2,)),
        ],
        compiler_params=pltpu.CompilerParams(
            collective_id=0, has_side_effects=True, vmem_limit_bytes=66 * 1024 * 1000),
    )(tok, ids, gates, hid)
    return result[None, None]


def solution(mesh):
    return jax.shard_map(
        functools.partial(on_device, mesh.shape["pipe"]),
        mesh=mesh,
        in_specs=(
            P(None, "pipe", "expert", None),
            P(None, "pipe", "expert", None),
            P(None, "pipe", "expert", None),
            P(None, "pipe", "expert", None, None),
        ),
        out_specs=P("pipe", "expert", None, None),
        check_vma=False,
    )
```

```python
import functools

import jax
import jax.numpy as jnp
from jax import lax
from jax.experimental import pallas as pl
from jax.experimental.pallas import tpu as pltpu
from jax.sharding import PartitionSpec as P

MESH = pl.DeviceIdType.MESH
SIDE = 4
CORES = 2
LANES = 128
WIDE = 2 * LANES
TRACKS = 3
LAGS = ((0, 3, 0), (1, 2, 1), (2, 1, 2), (4, 0, 3), (6, 0, 4))
VLIM = 50 * 1024 * 1024
BF = jnp.bfloat16
F32 = jnp.float32


def wrap(i):
    return lax.rem(i + 2 * SIDE, SIDE)


def kernel(ranks, cap, tok_ref, ids_ref, gate_ref, hid_ref, total,
           src, ring, pair, tiles, hid_t, hid_out, stage, select, own_tab, tab, tabs,
           to_far, to_sib,
           src_sem, x_sem, xt_sem, xh_sem, xsend_sem, stage_sem,
           ring_sem, own_sem, ring_send, pair_sem, pair_send,
           tab_sem, tab_own_sem, tab_send, tab_pair_sem, tab_pair_send,
           tile_sem, far_send, sib_send):
    tokens, width = tok_ref.shape[1], tok_ref.shape[2]
    slots, units = hid_ref.shape[1], hid_ref.shape[2]
    half = width // CORES
    chunks = half // WIDE
    steps = 2 * chunks
    both = CORES * cap
    piece = units // SIDE

    rank = lax.axis_index("pipe")
    expert = lax.axis_index("expert")
    c = lax.rem(expert, CORES)
    y = lax.rem(expert // CORES, SIDE)
    z = expert // (CORES * SIDE)
    mine_a = (1 - c) * z + c * y
    mine_b = (1 - c) * y + c * z
    step_a = lax.rem(mine_b, 2)
    near = wrap(mine_b + 1 - 2 * step_a)
    far = wrap(mine_b - 1 + 2 * step_a)

    def at(z_, y_, core):
        return {"pipe": rank, "expert": (z_ * SIDE + y_) * CORES + core}

    def at_ab(a_, b_, core):
        return at((1 - c) * a_ + c * b_, (1 - c) * b_ + c * a_, core)

    def expert_ab(a_, b_, core):
        return (((1 - c) * a_ + c * b_) * SIDE + (1 - c) * b_ + c * a_) * CORES + core

    sibling = at(z, y, 1 - c)
    mirror = {"pipe": ranks - 1 - rank, "expert": expert}

    def send(s_ref, d_ref, s_sem, r_sem, dev):
        pltpu.make_async_remote_copy(
            src_ref=s_ref, dst_ref=d_ref, send_sem=s_sem, recv_sem=r_sem,
            device_id=dev, device_id_type=MESH).start()

    def await_bytes(ref, sem):
        pltpu.make_async_copy(ref, ref, sem).wait()

    first = pltpu.make_async_copy(tok_ref.at[0], src.at[0], src_sem)
    first.start()

    def load_hidden(n):
        d, part = (1, n) if n < slots // WIDE else (0, n - slots // WIDE)
        return pltpu.make_async_copy(
            hid_ref.at[d, pl.ds(part * WIDE, WIDE)], stage.at[n % 2], stage_sem.at[n % 2])

    load_hidden(0).start()
    load_hidden(1).start()

    barrier = pltpu.get_barrier_semaphore()
    friends = [sibling, mirror]
    for core in range(CORES):
        for turn in (1, SIDE - 1):
            friends.append(at(wrap(z + turn), y, core))
            friends.append(at(z, wrap(y + turn), core))
    for friend in friends:
        pl.semaphore_signal(barrier, inc=1, device_id=friend, device_id_type=MESH)
    pl.semaphore_wait(barrier, len(friends))

    for k in range(chunks):
        for h in range(CORES):
            cols = pl.ds(h * half + k * WIDE, WIDE)
            send(tok_ref.at[1, :, cols], src.at[1, :, cols], xsend_sem.at[0], x_sem.at[k], mirror)

    e_row = lax.broadcasted_iota(jnp.int32, (SIDE * SIDE * CORES, tokens), 0)
    before = (lax.broadcasted_iota(jnp.int32, (tokens, tokens), 0)
              < lax.broadcasted_iota(jnp.int32, (tokens, tokens), 1)).astype(F32).astype(BF)
    for d in range(2):
        ids = ids_ref[d]
        top = ids.shape[0]
        named = jnp.zeros(e_row.shape, F32)
        for j in range(top):
            named += jnp.where(e_row == ids[j:j + 1, :], 1.0, 0.0)
        earlier = jnp.dot(named.astype(BF), before, preferred_element_type=F32)
        spots = [jnp.sum(jnp.where(e_row == ids[j:j + 1, :], earlier, 0.0), axis=0, keepdims=True)
                 for j in range(top)]
        into = tab.at[0] if d == 0 else own_tab
        into[0] = ids.astype(F32) * cap + jnp.concatenate(spots, axis=0)
        into[1] = gate_ref[d].astype(F32) / 64.0

    first.wait()

    def ring_out(source, dest, sems, send_sem, own, cols_of):
        for h in range(CORES):
            a_h = z if h == 0 else y
            for turn in (1, -1):
                dev = at(wrap(z + turn), y, 0) if h == 0 else at(z, wrap(y + turn), 1)
                which = 2 * c if turn == 1 else 2 - c
                send(cols_of(source, h), dest.at[a_h * CORES + c], send_sem, sems.at[which], dev)
        sib_a = c * z + (1 - c) * y
        send(cols_of(source, 1 - c), dest.at[sib_a * CORES + c], send_sem, sems.at[2], sibling)
        pltpu.make_async_copy(cols_of(source, c), dest.at[mine_a * CORES + c], own).start()

    def ring_on(dest, sems, send_sem):
        for turn, core in ((1, 0), (-1, 1)):
            part = dest.at[wrap(mine_a - turn) * CORES + core]
            await_bytes(part, sems.at[core])
            send(part, part, send_sem, sems.at[2], at_ab(wrap(mine_a + turn), mine_b, c))

    def step_cols(k):
        return lambda ref, h: ref.at[:, pl.ds(pl.multiple_of(h * half + k * WIDE, LANES), WIDE)]

    def stage_a(s):
        d, k = s // chunks, lax.rem(s, chunks)

        @pl.when(d == 1)
        def _():
            await_bytes(src.at[1, :, pl.ds(0, 2 * WIDE)], x_sem.at[k])

        @pl.when(k == 0)
        def _():
            @pl.when(d == 1)
            def _():
                await_bytes(tab.at[1], xt_sem)
            ring_out(tab.at[d], tabs.at[d, 0], tab_sem.at[d], tab_send.at[d], tab_own_sem.at[d],
                     lambda ref, h: ref)

        ring_out(src.at[d], ring.at[s], ring_sem.at[s], ring_send.at[s], own_sem.at[s], step_cols(k))

    def stage_b(s):
        d, k = s // chunks, lax.rem(s, chunks)

        @pl.when(k == 0)
        def _():
            ring_on(tabs.at[d, 0], tab_sem.at[d], tab_send.at[d])

        ring_on(ring.at[s], ring_sem.at[s], ring_send.at[s])

    def stage_c(s):
        d, k = s // chunks, lax.rem(s, chunks)

        @pl.when(k == 0)
        def _():
            await_bytes(tabs.at[d, 0, pl.ds(0, 5)], tab_sem.at[d, 2])
            await_bytes(tabs.at[d, 0, 0], tab_own_sem.at[d])
            for p, friend in ((0, near), (1, far)):
                send(tabs.at[d, 0], tabs.at[d, 1 + p], tab_pair_send.at[d], tab_pair_sem.at[d],
                     at_ab(mine_a, friend, c))

        await_bytes(ring.at[s, pl.ds(0, 5)], ring_sem.at[s, 2])
        await_bytes(ring.at[s, 0], own_sem.at[s])
        for p, friend in ((0, near), (1, far)):
            send(ring.at[s, :, :, pl.ds(p * LANES, LANES)], pair.at[s, p], pair_send.at[s],
                 pair_sem.at[s], at_ab(mine_a, friend, c))

    row = lax.broadcasted_iota(jnp.int32, (both, CORES * tokens), 0)
    lane = lax.broadcasted_iota(jnp.int32, (both, CORES * tokens), 1)
    target = jnp.where((row < cap) == (lane < tokens), jnp.where(row < cap, row, row - cap), -2).astype(F32)

    def select_rows(d, where_, a_, e):
        found = []
        for core in range(CORES):
            t = tabs.at[d, where_, a_ * CORES + core]
            local = t[0] - (e * cap).astype(F32)
            hit = (local >= 0.0) & (local < cap)
            spot = jnp.sum(jnp.where(hit, local + 1.0, 0.0), axis=0, keepdims=True) - 1.0
            weight = jnp.sum(jnp.where(hit, t[1], 0.0), axis=0, keepdims=True)
            found.append((spot, weight))
        spot = jnp.concatenate([f[0] for f in found], axis=1)
        weight = jnp.concatenate([f[1] for f in found], axis=1)
        return jnp.where(spot == target, weight, 0.0).astype(BF)

    own2 = [(mine_b, c), (mine_b, 1 - c)]
    near2 = [(near, 0), (near, 1)]
    far2 = [(far, 0), (far, 1)]
    plan = [(0, x) for x in near2 + own2 + far2] + [(1, x) for x in own2 + far2] + [(2, x) for x in near2 + own2]

    def build_select(d):
        @pl.loop(0, SIDE)
        def _(a_):
            for n, (where_, (b_, core)) in enumerate(plan):
                select[a_, pl.ds(n * both, both), :] = select_rows(d, where_, a_, expert_ab(mine_a, b_, core))

    lead = {(0, 0): 2, (0, 1): 6, (1, 0): 0, (1, 1): 10}

    def stage_d(s):
        d, k = s // chunks, lax.rem(s, chunks)
        track = lax.rem(s, TRACKS)

        @pl.when(k == 0)
        def _():
            await_bytes(tabs.at[d, pl.ds(1, 2)], tab_pair_sem.at[d])
            build_select(d)

        @pl.when(s >= TRACKS)
        def _():
            await_bytes(to_far.at[track], far_send.at[track])
            await_bytes(to_sib.at[track], sib_send.at[track])

        await_bytes(ring.at[s], pair_sem.at[s])
        for p in range(2):
            friend = near if p == 0 else far
            for b_at in range(2):
                b_ = mine_b if b_at == 0 else friend
                start = lead[(p, b_at)] * both

                @pl.loop(0, SIDE)
                def _(a_):
                    if b_at == 0:
                        rows = ring[s, pl.ds(a_ * CORES, CORES), :, p * LANES:(p + 1) * LANES]
                    else:
                        rows = pair[s, p, pl.ds(a_ * CORES, CORES)]
                    rows = rows.reshape(CORES * tokens, LANES)
                    got = jnp.dot(select[a_, pl.ds(start, 4 * both), :], rows,
                                  preferred_element_type=F32).astype(BF)
                    own_at = 0 if p == 0 else 2 * both
                    far_at = 2 * both if p == 0 else 0
                    z_, y_ = (1 - c) * a_ + c * b_, (1 - c) * b_ + c * a_
                    tiles[s * CORES + c, z_, y_, :, p * LANES:(p + 1) * LANES] = got[own_at:own_at + both]
                    to_sib[track, p, b_at, a_] = got[own_at + both:own_at + 2 * both]
                    for core in range(CORES):
                        to_far[track, p, core, b_at, a_] = got[far_at + core * both:far_at + (core + 1) * both]

        for h in range(CORES):
            @pl.when(c == h)
            def _():
                into = tiles.at[s * CORES + h]
                for p in range(2):
                    cols = pl.ds(p * LANES, LANES)
                    friend = near if p == 0 else far
                    other = far if p == 0 else near
                    for b_at in range(2):
                        b_ = mine_b if b_at == 0 else friend
                        part = into.at[:, b_, :, cols] if h == 0 else into.at[b_, :, :, cols]
                        for core in range(CORES):
                            send(to_far.at[track, p, core, b_at], part, far_send.at[track],
                                 tile_sem.at[s * CORES + h], at_ab(mine_a, other, core))
                        send(to_sib.at[track, p, b_at], part, sib_send.at[track],
                             tile_sem.at[s * CORES + h], sibling)

    def stage_e(s):
        d, k = s // chunks, lax.rem(s, chunks)
        await_bytes(tiles.at[0, pl.ds(0, 2)], tile_sem.at[s * CORES + c])
        await_bytes(tiles.at[0], tile_sem.at[s * CORES + 1 - c])

        @pl.when(s == chunks)
        def _():
            await_bytes(hid_t.at[1], xh_sem)

        def add_product(dest, prior):
            @pl.loop(0, CORES)
            def _(h):
                @pl.loop(0, SIDE)
                def _(f):
                    rows = pl.ds(f * piece, piece)
                    got = jnp.dot(hid_t[d, rows, :], tiles[s * CORES + h].reshape(slots, WIDE),
                                  preferred_element_type=F32)
                    if prior:
                        got = got + total[k * CORES + h, rows, :].astype(F32)
                    total[k * CORES + h, rows, :] = got.astype(BF)

        @pl.when(d == 0)
        def _():
            add_product(total, False)

        @pl.when(d == 1)
        def _():
            add_product(total, True)

    def transpose_hidden(d):
        parts = slots // WIDE
        for n in range((1 - d) * parts, (2 - d) * parts):
            load_hidden(n).wait()
            into = hid_out if n < parts else hid_t.at[0]
            part = n % parts

            @pl.loop(0, units // WIDE)
            def _(f):
                at_f = pl.multiple_of(f * WIDE, WIDE)
                into[pl.ds(at_f, WIDE), part * WIDE:(part + 1) * WIDE] = stage[n % 2, :, pl.ds(at_f, WIDE)].T

            if n + 2 < 2 * parts:
                load_hidden(n + 2).start()

    stage_a(jnp.int32(0))
    send(own_tab, tab.at[1], xsend_sem.at[1], xt_sem, mirror)
    stage_a(jnp.int32(1))
    stage_a(jnp.int32(2))
    stage_b(jnp.int32(0))
    transpose_hidden(1)
    send(hid_out, hid_t.at[1], xsend_sem.at[2], xh_sem, mirror)
    stage_b(jnp.int32(1))
    stage_c(jnp.int32(0))
    transpose_hidden(0)

    def turn(i, carry):
        for lag, skip, work in LAGS:
            @pl.when((i - lag >= skip) & (i - lag < steps))
            def _():
                (stage_a, stage_b, stage_c, stage_d, stage_e)[work](i - lag)
        return carry

    lax.fori_loop(3, steps + LAGS[-1][0], turn, 0)

    for track in range(TRACKS):
        await_bytes(to_far.at[track], far_send.at[track])
        await_bytes(to_sib.at[track], sib_send.at[track])
    await_bytes(src.at[1], xsend_sem.at[0])
    await_bytes(own_tab, xsend_sem.at[1])
    await_bytes(hid_out, xsend_sem.at[2])

    @pl.loop(0, steps)
    def _(s):
        await_bytes(ring.at[s, pl.ds(0, 7)], ring_send.at[s])
        await_bytes(ring.at[s], pair_send.at[s])

    for d in range(2):
        await_bytes(tabs.at[d, 0, pl.ds(0, 7)], tab_send.at[d])
        await_bytes(tabs.at[d, pl.ds(1, 2)], tab_pair_send.at[d])


def finish(total, out_ref, sem):
    count, units, wide = total.shape
    chunks = count // CORES

    def put(n):
        k, h = n // CORES, n % CORES
        cols = pl.ds(h * chunks * wide + k * wide, wide)
        return pltpu.make_async_copy(total.at[n], out_ref.at[:, cols], sem.at[n])

    for n in range(count):
        put(n).start()
    for n in range(count):
        put(n).wait()


def on_device(ranks, grad_rows, expert_ids, gate_buckets, saved_hidden):
    tok, hid = grad_rows[:, 0], saved_hidden[:, 0, 0]
    ids = expert_ids[:, 0].transpose(0, 2, 1)
    gates = gate_buckets[:, 0].transpose(0, 2, 1)
    tokens, width = tok.shape[1:]
    top = ids.shape[1]
    slots, units = hid.shape[1:]
    cap = slots // (SIDE * SIDE * CORES)
    both = CORES * cap
    steps = width // WIDE
    dma = pltpu.SemaphoreType.DMA
    (total,) = pl.pallas_call(
        functools.partial(kernel, ranks, cap),
        out_shape=[
            pltpu.VMEM((steps, units, WIDE), BF),
        ],
        in_specs=[
            pl.BlockSpec(memory_space=pl.ANY),
            pl.BlockSpec(memory_space=pltpu.VMEM),
            pl.BlockSpec(memory_space=pltpu.VMEM),
            pl.BlockSpec(memory_space=pl.ANY),
        ],
        out_specs=[pl.BlockSpec(memory_space=pltpu.VMEM)],
        scratch_shapes=[
            pltpu.VMEM((2, tokens, width), BF),
            pltpu.VMEM((steps, SIDE * CORES, tokens, WIDE), BF),
            pltpu.VMEM((steps, 2, SIDE * CORES, tokens, LANES), BF),
            pltpu.VMEM((steps * CORES, SIDE, SIDE, both, WIDE), BF),
            pltpu.VMEM((2, units, slots), BF),
            pltpu.VMEM((units, slots), BF),
            pltpu.VMEM((2, WIDE, units), BF),
            pltpu.VMEM((SIDE, 14 * both, CORES * tokens), BF),
            pltpu.VMEM((2, top, tokens), F32),
            pltpu.VMEM((2, 2, top, tokens), F32),
            pltpu.VMEM((2, 3, SIDE * CORES, 2, top, tokens), F32),
            pltpu.VMEM((TRACKS, 2, CORES, 2, SIDE, both, LANES), BF),
            pltpu.VMEM((TRACKS, 2, 2, SIDE, both, LANES), BF),
            dma, dma((steps // 2,)), dma, dma, dma((3,)), dma((2,)),
            dma((steps, 3)), dma((steps,)), dma((steps,)), dma((steps,)), dma((steps,)),
            dma((2, 3)), dma((2,)), dma((2,)), dma((2,)), dma((2,)),
            dma((steps * CORES,)), dma((TRACKS,)), dma((TRACKS,)),
        ],
        compiler_params=pltpu.CompilerParams(
            collective_id=0, has_side_effects=True, vmem_limit_bytes=VLIM),
    )(tok, ids, gates, hid)
    result = pl.pallas_call(
        finish,
        out_shape=jax.ShapeDtypeStruct((units, width), BF),
        in_specs=[pl.BlockSpec(memory_space=pltpu.VMEM)],
        out_specs=pl.BlockSpec(memory_space=pl.ANY),
        scratch_shapes=[dma((steps,))],
        compiler_params=pltpu.CompilerParams(vmem_limit_bytes=4 * 1024 * 1024),
    )(total)
    return result[None, None]


def solution(mesh):
    return jax.shard_map(
        functools.partial(on_device, mesh.shape["pipe"]),
        mesh=mesh,
        in_specs=(
            P(None, "pipe", "expert", None),
            P(None, "pipe", "expert", None),
            P(None, "pipe", "expert", None),
            P(None, "pipe", "expert", None, None),
        ),
        out_specs=P("pipe", "expert", None, None),
        check_vma=False,
    )
```

```python
import functools

import jax
import jax.numpy as jnp
from jax import lax
from jax.experimental import pallas as pl
from jax.experimental.pallas import tpu as pltpu
from jax.sharding import PartitionSpec as P

MESH = pl.DeviceIdType.MESH
SIDE = 4
CORES = 2
LANES = 128
WIDE = 2 * LANES
TRACKS = 3
AHEAD = 7
LAGS = ((0, 7, 0), (5, 2, 1), (6, 1, 2), (8, 0, 3), (10, 0, 4))
VLIM = 46 * 1024 * 1024
BF = jnp.bfloat16
F32 = jnp.float32


def wrap(i):
    return lax.rem(i + 2 * SIDE, SIDE)


def kernel(ranks, cap, tok_ref, ids_ref, gate_ref, hid_ref, total, last, hid_two,
           src, ring, pair, tiles, hid_one, hid_out, stage, select, own_tab, tab, tabs,
           to_far, to_sib,
           x_sem, xt_sem, xh_sem, xsend_sem, stage_sem,
           ring_sem, own_sem, ring_send, pair_sem, pair_send,
           tab_sem, tab_own_sem, tab_send, tab_pair_sem, tab_pair_send,
           tile_sem, far_send, sib_send):
    tokens, width = tok_ref.shape[1], tok_ref.shape[2]
    slots, units = hid_ref.shape[1], hid_ref.shape[2]
    half = width // CORES
    chunks = half // WIDE
    steps = 2 * chunks
    both = CORES * cap
    piece = units // SIDE

    rank = lax.axis_index("pipe")
    expert = lax.axis_index("expert")
    c = lax.rem(expert, CORES)
    y = lax.rem(expert // CORES, SIDE)
    z = expert // (CORES * SIDE)
    mine_a = (1 - c) * z + c * y
    mine_b = (1 - c) * y + c * z
    step_a = lax.rem(mine_b, 2)
    near = wrap(mine_b + 1 - 2 * step_a)
    far = wrap(mine_b - 1 + 2 * step_a)

    def at(z_, y_, core):
        return {"pipe": rank, "expert": (z_ * SIDE + y_) * CORES + core}

    def at_ab(a_, b_, core):
        return at((1 - c) * a_ + c * b_, (1 - c) * b_ + c * a_, core)

    def expert_ab(a_, b_, core):
        return (((1 - c) * a_ + c * b_) * SIDE + (1 - c) * b_ + c * a_) * CORES + core

    sibling = at(z, y, 1 - c)
    mirror = {"pipe": ranks - 1 - rank, "expert": expert}

    def send(s_ref, d_ref, s_sem, r_sem, dev):
        pltpu.make_async_remote_copy(
            src_ref=s_ref, dst_ref=d_ref, send_sem=s_sem, recv_sem=r_sem,
            device_id=dev, device_id_type=MESH).start()

    def await_bytes(ref, sem):
        pltpu.make_async_copy(ref, ref, sem).wait()

    def load_hidden(n):
        d, part = (1, n) if n < slots // WIDE else (0, n - slots // WIDE)
        return pltpu.make_async_copy(
            hid_ref.at[d, pl.ds(part * WIDE, WIDE)], stage.at[n % 2], stage_sem.at[n % 2])

    load_hidden(0).start()
    load_hidden(1).start()

    barrier = pltpu.get_barrier_semaphore()
    friends = [sibling, mirror]
    for core in range(CORES):
        for turn in (1, SIDE - 1):
            friends.append(at(wrap(z + turn), y, core))
            friends.append(at(z, wrap(y + turn), core))
    for friend in friends:
        pl.semaphore_signal(barrier, inc=1, device_id=friend, device_id_type=MESH)

    e_row = lax.broadcasted_iota(jnp.int32, (SIDE * SIDE * CORES, tokens), 0)
    before = (lax.broadcasted_iota(jnp.int32, (tokens, tokens), 0)
              < lax.broadcasted_iota(jnp.int32, (tokens, tokens), 1)).astype(F32).astype(BF)
    for d in range(2):
        ids = ids_ref[d]
        top = ids.shape[0]
        named = jnp.zeros(e_row.shape, F32)
        for j in range(top):
            named += jnp.where(e_row == ids[j:j + 1, :], 1.0, 0.0)
        earlier = jnp.dot(named.astype(BF), before, preferred_element_type=F32)
        spots = [jnp.sum(jnp.where(e_row == ids[j:j + 1, :], earlier, 0.0), axis=0, keepdims=True)
                 for j in range(top)]
        into = tab.at[0] if d == 0 else own_tab
        into[0] = ids.astype(F32) * cap + jnp.concatenate(spots, axis=0)
        into[1] = gate_ref[d].astype(F32) / 64.0

    pl.semaphore_wait(barrier, len(friends))

    def ring_out(source, dest, sems, send_sem, own, cols_of):
        for h in range(CORES):
            a_h = z if h == 0 else y
            for turn in (1, -1):
                dev = at(wrap(z + turn), y, 0) if h == 0 else at(z, wrap(y + turn), 1)
                which = 2 * c if turn == 1 else 2 - c
                send(cols_of(source, h), dest.at[a_h * CORES + c], send_sem, sems.at[which], dev)
        sib_a = c * z + (1 - c) * y
        send(cols_of(source, 1 - c), dest.at[sib_a * CORES + c], send_sem, sems.at[2], sibling)
        pltpu.make_async_copy(cols_of(source, c), dest.at[mine_a * CORES + c], own).start()

    def ring_on(dest, sems, send_sem):
        for turn, core in ((1, 0), (-1, 1)):
            part = dest.at[wrap(mine_a - turn) * CORES + core]
            await_bytes(part, sems.at[core])
            send(part, part, send_sem, sems.at[2], at_ab(wrap(mine_a + turn), mine_b, c))

    def step_cols(k):
        return lambda ref, h: ref.at[:, pl.ds(pl.multiple_of(h * half + k * WIDE, LANES), WIDE)]

    def tables_out(d):
        ring_out(tab.at[d], tabs.at[d, 0], tab_sem.at[d], tab_send.at[d], tab_own_sem.at[d], lambda ref, h: ref)

    def rows_out(s, source, k):
        ring_out(source, ring.at[s], ring_sem.at[s], ring_send.at[s], own_sem.at[s], step_cols(k))

    def stage_a(s):
        k = s - chunks

        @pl.when(k < 0)
        def _():
            rows_out(s, tok_ref.at[0], s)

        @pl.when(k == 0)
        def _():
            await_bytes(tab.at[1], xt_sem)
            tables_out(1)

        @pl.when(k >= 0)
        def _():
            await_bytes(src.at[:, pl.ds(0, 2 * WIDE)], x_sem.at[k])
            rows_out(s, src, k)

    def stage_b(s):
        d, k = s // chunks, lax.rem(s, chunks)

        @pl.when(k == 0)
        def _():
            ring_on(tabs.at[d, 0], tab_sem.at[d], tab_send.at[d])

        ring_on(ring.at[s], ring_sem.at[s], ring_send.at[s])

    def stage_c(s):
        d, k = s // chunks, lax.rem(s, chunks)

        @pl.when(k == 0)
        def _():
            await_bytes(tabs.at[d, 0, pl.ds(0, 5)], tab_sem.at[d, 2])
            await_bytes(tabs.at[d, 0, 0], tab_own_sem.at[d])
            for p, friend in ((0, near), (1, far)):
                send(tabs.at[d, 0], tabs.at[d, 1 + p], tab_pair_send.at[d], tab_pair_sem.at[d],
                     at_ab(mine_a, friend, c))

        await_bytes(ring.at[s, pl.ds(0, 5)], ring_sem.at[s, 2])
        await_bytes(ring.at[s, 0], own_sem.at[s])
        for p, friend in ((0, near), (1, far)):
            send(ring.at[s, :, :, pl.ds(p * LANES, LANES)], pair.at[s, p], pair_send.at[s],
                 pair_sem.at[s], at_ab(mine_a, friend, c))

    row = lax.broadcasted_iota(jnp.int32, (both, CORES * tokens), 0)
    lane = lax.broadcasted_iota(jnp.int32, (both, CORES * tokens), 1)
    target = jnp.where((row < cap) == (lane < tokens), jnp.where(row < cap, row, row - cap), -2).astype(F32)

    def select_rows(d, where_, a_, e):
        found = []
        for core in range(CORES):
            t = tabs.at[d, where_, a_ * CORES + core]
            local = t[0] - (e * cap).astype(F32)
            hit = (local >= 0.0) & (local < cap)
            spot = jnp.sum(jnp.where(hit, local + 1.0, 0.0), axis=0, keepdims=True) - 1.0
            weight = jnp.sum(jnp.where(hit, t[1], 0.0), axis=0, keepdims=True)
            found.append((spot, weight))
        spot = jnp.concatenate([f[0] for f in found], axis=1)
        weight = jnp.concatenate([f[1] for f in found], axis=1)
        return jnp.where(spot == target, weight, 0.0).astype(BF)

    own2 = [(mine_b, c), (mine_b, 1 - c)]
    near2 = [(near, 0), (near, 1)]
    far2 = [(far, 0), (far, 1)]
    plan = [(0, x) for x in near2 + own2 + far2] + [(1, x) for x in own2 + far2] + [(2, x) for x in near2 + own2]

    def build_select(d):
        @pl.loop(0, SIDE)
        def _(a_):
            for n, (where_, (b_, core)) in enumerate(plan):
                select[a_, pl.ds(n * both, both), :] = select_rows(d, where_, a_, expert_ab(mine_a, b_, core))

    lead = {(0, 0): 2, (0, 1): 6, (1, 0): 0, (1, 1): 10}

    def stage_d(s):
        d, k = s // chunks, lax.rem(s, chunks)
        track = lax.rem(s, TRACKS)

        @pl.when(k == 0)
        def _():
            await_bytes(tabs.at[d, pl.ds(1, 2)], tab_pair_sem.at[d])
            build_select(d)

        @pl.when(s >= TRACKS)
        def _():
            await_bytes(to_far.at[track], far_send.at[track])
            await_bytes(to_sib.at[track], sib_send.at[track])

        await_bytes(ring.at[s], pair_sem.at[s])
        for p in range(2):
            friend = near if p == 0 else far
            for b_at in range(2):
                b_ = mine_b if b_at == 0 else friend
                start = lead[(p, b_at)] * both

                @pl.loop(0, SIDE)
                def _(a_):
                    if b_at == 0:
                        rows = ring[s, pl.ds(a_ * CORES, CORES), :, p * LANES:(p + 1) * LANES]
                    else:
                        rows = pair[s, p, pl.ds(a_ * CORES, CORES)]
                    rows = rows.reshape(CORES * tokens, LANES)
                    got = jnp.dot(select[a_, pl.ds(start, 4 * both), :], rows,
                                  preferred_element_type=F32).astype(BF)
                    own_at = 0 if p == 0 else 2 * both
                    far_at = 2 * both if p == 0 else 0
                    z_, y_ = (1 - c) * a_ + c * b_, (1 - c) * b_ + c * a_
                    kept = got[own_at:own_at + both]

                    @pl.when(s < steps - 1)
                    def _():
                        tiles[s * CORES + c, z_, y_, :, p * LANES:(p + 1) * LANES] = kept

                    @pl.when(s == steps - 1)
                    def _():
                        last[c, z_, y_, :, p * LANES:(p + 1) * LANES] = kept

                    to_sib[track, p, b_at, a_] = got[own_at + both:own_at + 2 * both]
                    for core in range(CORES):
                        to_far[track, p, core, b_at, a_] = got[far_at + core * both:far_at + (core + 1) * both]

        for final_step, goal in ((s < steps - 1, lambda h: tiles.at[s * CORES + h]),
                                 (s == steps - 1, lambda h: last.at[h])):
            for h in range(CORES):
                @pl.when((c == h) & final_step)
                def _():
                    into = goal(h)
                    for p in range(2):
                        cols = pl.ds(p * LANES, LANES)
                        friend = near if p == 0 else far
                        other = far if p == 0 else near
                        for b_at in range(2):
                            b_ = mine_b if b_at == 0 else friend
                            part = into.at[:, b_, :, cols] if h == 0 else into.at[b_, :, :, cols]
                            for core in range(CORES):
                                send(to_far.at[track, p, core, b_at], part, far_send.at[track],
                                     tile_sem.at[s * CORES + h], at_ab(mine_a, other, core))
                            send(to_sib.at[track, p, b_at], part, sib_send.at[track],
                                 tile_sem.at[s * CORES + h], sibling)

    def stage_e(s):
        d, k = s // chunks, lax.rem(s, chunks)
        await_bytes(tiles.at[0, pl.ds(0, SIDE // 2)], tile_sem.at[s * CORES + c])
        await_bytes(tiles.at[0], tile_sem.at[s * CORES + 1 - c])

        @pl.when(s == chunks)
        def _():
            await_bytes(hid_two, xh_sem)

        def add_product(hid, prior):
            @pl.loop(0, CORES)
            def _(h):
                @pl.loop(0, SIDE)
                def _(f):
                    rows = pl.ds(f * piece, piece)
                    got = jnp.dot(hid[rows, :], tiles[s * CORES + h].reshape(slots, WIDE),
                                  preferred_element_type=F32)
                    if prior:
                        got = got + total[k * CORES + h, rows, :].astype(F32)
                    total[k * CORES + h, rows, :] = got.astype(BF)

        @pl.when(d == 0)
        def _():
            add_product(hid_one, False)

        @pl.when((d == 1) & (s < steps - 1))
        def _():
            add_product(hid_two, True)

    def transpose_hidden(d):
        parts = slots // WIDE
        for n in range((1 - d) * parts, (2 - d) * parts):
            load_hidden(n).wait()
            into = hid_out if n < parts else hid_one
            part = n % parts

            @pl.loop(0, units // WIDE)
            def _(f):
                at_f = pl.multiple_of(f * WIDE, WIDE)
                into[pl.ds(at_f, WIDE), part * WIDE:(part + 1) * WIDE] = stage[n % 2, :, pl.ds(at_f, WIDE)].T

            if n + 2 < 2 * parts:
                load_hidden(n + 2).start()

    for s in range(AHEAD):
        rows_out(s, tok_ref.at[0], s)
        if s == 0:
            tables_out(0)
            send(own_tab, tab.at[1], xsend_sem.at[1], xt_sem, mirror)
    for k in range(chunks):
        for h in range(CORES):
            cols = pl.ds(h * half + k * WIDE, WIDE)
            send(tok_ref.at[1, :, cols], src.at[:, cols], xsend_sem.at[0], x_sem.at[k], mirror)
    stage_b(jnp.int32(0))
    transpose_hidden(1)
    send(hid_out, hid_two, xsend_sem.at[2], xh_sem, mirror)
    stage_b(jnp.int32(1))
    stage_c(jnp.int32(0))
    transpose_hidden(0)

    def turn(i, carry):
        for lag, skip, work in LAGS:
            @pl.when((i - lag >= skip) & (i - lag < steps))
            def _():
                (stage_a, stage_b, stage_c, stage_d, stage_e)[work](i - lag)
        return carry

    lax.fori_loop(AHEAD, steps + LAGS[-1][0], turn, 0)

    for track in range(TRACKS):
        await_bytes(to_far.at[track], far_send.at[track])
        await_bytes(to_sib.at[track], sib_send.at[track])
    await_bytes(src, xsend_sem.at[0])
    await_bytes(own_tab, xsend_sem.at[1])
    await_bytes(hid_out, xsend_sem.at[2])

    @pl.loop(0, steps)
    def _(s):
        await_bytes(ring.at[s, pl.ds(0, 7)], ring_send.at[s])
        await_bytes(ring.at[s], pair_send.at[s])

    for d in range(2):
        await_bytes(tabs.at[d, 0, pl.ds(0, 7)], tab_send.at[d])
        await_bytes(tabs.at[d, pl.ds(1, 2)], tab_pair_send.at[d])


def finish(total, last, hid_two, out_ref, made, sem):
    count, units, wide = total.shape
    slots = hid_two.shape[1]
    chunks = count // CORES
    piece = units // SIDE

    def put(k, h):
        cols = pl.ds(h * chunks * wide + k * wide, wide)
        rows = total.at[k * CORES + h] if k < chunks - 1 else made.at[h]
        return pltpu.make_async_copy(rows, out_ref.at[:, cols], sem.at[k * CORES + h])

    for k in range(chunks - 1):
        for h in range(CORES):
            put(k, h).start()
    for h in range(CORES):
        @pl.loop(0, SIDE)
        def _(f):
            rows = pl.ds(f * piece, piece)
            got = jnp.dot(hid_two[rows, :], last[h].reshape(slots, wide), preferred_element_type=F32)
            made[h, rows, :] = (got + total[count - CORES + h, rows, :].astype(F32)).astype(BF)
        put(chunks - 1, h).start()
    for k in range(chunks):
        for h in range(CORES):
            put(k, h).wait()


def on_device(ranks, grad_rows, expert_ids, gate_buckets, saved_hidden):
    tok, hid = grad_rows[:, 0], saved_hidden[:, 0, 0]
    ids = expert_ids[:, 0].transpose(0, 2, 1)
    gates = gate_buckets[:, 0].transpose(0, 2, 1)
    tokens, width = tok.shape[1:]
    top = ids.shape[1]
    slots, units = hid.shape[1:]
    cap = slots // (SIDE * SIDE * CORES)
    both = CORES * cap
    steps = width // WIDE
    dma = pltpu.SemaphoreType.DMA
    total, last, hid_two = pl.pallas_call(
        functools.partial(kernel, ranks, cap),
        out_shape=[
            pltpu.VMEM((steps, units, WIDE), BF),
            pltpu.VMEM((CORES, SIDE, SIDE, both, WIDE), BF),
            pltpu.VMEM((units, slots), BF),
        ],
        in_specs=[
            pl.BlockSpec(memory_space=pl.ANY),
            pl.BlockSpec(memory_space=pltpu.VMEM),
            pl.BlockSpec(memory_space=pltpu.VMEM),
            pl.BlockSpec(memory_space=pl.ANY),
        ],
        out_specs=[pl.BlockSpec(memory_space=pltpu.VMEM)] * 3,
        scratch_shapes=[
            pltpu.VMEM((tokens, width), BF),
            pltpu.VMEM((steps, SIDE * CORES, tokens, WIDE), BF),
            pltpu.VMEM((steps, 2, SIDE * CORES, tokens, LANES), BF),
            pltpu.VMEM(((steps - 1) * CORES, SIDE, SIDE, both, WIDE), BF),
            pltpu.VMEM((units, slots), BF),
            pltpu.VMEM((units, slots), BF),
            pltpu.VMEM((2, WIDE, units), BF),
            pltpu.VMEM((SIDE, 14 * both, CORES * tokens), BF),
            pltpu.VMEM((2, top, tokens), F32),
            pltpu.VMEM((2, 2, top, tokens), F32),
            pltpu.VMEM((2, 3, SIDE * CORES, 2, top, tokens), F32),
            pltpu.VMEM((TRACKS, 2, CORES, 2, SIDE, both, LANES), BF),
            pltpu.VMEM((TRACKS, 2, 2, SIDE, both, LANES), BF),
            dma((steps // 2,)), dma, dma, dma((3,)), dma((2,)),
            dma((steps, 3)), dma((steps,)), dma((steps,)), dma((steps,)), dma((steps,)),
            dma((2, 3)), dma((2,)), dma((2,)), dma((2,)), dma((2,)),
            dma((steps * CORES,)), dma((TRACKS,)), dma((TRACKS,)),
        ],
        compiler_params=pltpu.CompilerParams(
            collective_id=0, has_side_effects=True, vmem_limit_bytes=VLIM),
    )(tok, ids, gates, hid)
    result = pl.pallas_call(
        finish,
        out_shape=jax.ShapeDtypeStruct((units, width), BF),
        in_specs=[pl.BlockSpec(memory_space=pltpu.VMEM)] * 3,
        out_specs=pl.BlockSpec(memory_space=pl.ANY),
        scratch_shapes=[pltpu.VMEM((CORES, units, WIDE), BF), dma((steps,))],
        compiler_params=pltpu.CompilerParams(vmem_limit_bytes=4 * 1024 * 1024),
    )(total, last, hid_two)
    return result[None, None]


def solution(mesh):
    return jax.shard_map(
        functools.partial(on_device, mesh.shape["pipe"]),
        mesh=mesh,
        in_specs=(
            P(None, "pipe", "expert", None),
            P(None, "pipe", "expert", None),
            P(None, "pipe", "expert", None),
            P(None, "pipe", "expert", None, None),
        ),
        out_specs=P("pipe", "expert", None, None),
        check_vma=False,
    )
```

```python
import functools

import jax
import jax.numpy as jnp
from jax import lax
from jax.experimental import pallas as pl
from jax.experimental.pallas import tpu as pltpu
from jax.sharding import PartitionSpec as P

MESH = pl.DeviceIdType.MESH
SIDE = 4
CORES = 2
LANES = 128
WIDE = 2 * LANES
TRACKS = 3
AHEAD = 7
LAGS = ((0, 7, 0), (5, 2, 1), (6, 1, 2), (7, 0, 3), (9, 0, 4))
VLIM = 46 * 1024 * 1024
INNER = ((0, 0), (0, -1), (-1, -1), (1, 0), (1, 1), (2, 1))
LEAVES = (((0, 1), (-1, 0)), ((0, -1), (1, 0)), ((-1, 0), (0, -1)), ((1, 0),), ((0, 1),), ((0, 1), (1, 0)))
SIGNS = (1, -1)
BF = jnp.bfloat16
F32 = jnp.float32


def wrap(i):
    return lax.rem(i + 2 * SIDE, SIDE)


def kernel(ranks, cap, tok_ref, ids_ref, gate_ref, hid_ref, total, last, hid_two,
           src, full, tiles, hid_one, hid_out, stage, select, own_tab, tab, tabs,
           to_far, to_sib,
           x_sem, xt_sem, xh_sem, xsend_sem, stage_sem,
           own_sem, sib_sem, hop_sem, hop_send,
           tab_own_sem, tab_sib_sem, tab_hop_sem, tab_hop_send,
           tile_sem, far_send, sib_send):
    tokens, width = tok_ref.shape[1], tok_ref.shape[2]
    slots, units = hid_ref.shape[1], hid_ref.shape[2]
    half = width // CORES
    chunks = half // WIDE
    steps = 2 * chunks
    both = CORES * cap
    piece = units // SIDE

    rank = lax.axis_index("pipe")
    expert = lax.axis_index("expert")
    c = lax.rem(expert, CORES)
    y = lax.rem(expert // CORES, SIDE)
    z = expert // (CORES * SIDE)
    mine_a = (1 - c) * z + c * y
    mine_b = (1 - c) * y + c * z
    def at(z_, y_, core):
        return {"pipe": rank, "expert": (z_ * SIDE + y_) * CORES + core}

    def at_ab(a_, b_, core):
        return at((1 - c) * a_ + c * b_, (1 - c) * b_ + c * a_, core)

    def expert_ab(a_, b_, core):
        return (((1 - c) * a_ + c * b_) * SIDE + (1 - c) * b_ + c * a_) * CORES + core

    sibling = at(z, y, 1 - c)
    mirror = {"pipe": ranks - 1 - rank, "expert": expert}

    def send(s_ref, d_ref, s_sem, r_sem, dev):
        pltpu.make_async_remote_copy(
            src_ref=s_ref, dst_ref=d_ref, send_sem=s_sem, recv_sem=r_sem,
            device_id=dev, device_id_type=MESH).start()

    def await_bytes(ref, sem):
        pltpu.make_async_copy(ref, ref, sem).wait()

    def load_hidden(n):
        d, part = (1, n) if n < slots // WIDE else (0, n - slots // WIDE)
        return pltpu.make_async_copy(
            hid_ref.at[d, pl.ds(part * WIDE, WIDE)], stage.at[n % 2], stage_sem.at[n % 2])

    load_hidden(0).start()
    load_hidden(1).start()

    barrier = pltpu.get_barrier_semaphore()
    friends = [sibling, mirror]
    for core in range(CORES):
        for turn in (1, SIDE - 1):
            friends.append(at(wrap(z + turn), y, core))
            friends.append(at(z, wrap(y + turn), core))
    for friend in friends:
        pl.semaphore_signal(barrier, inc=1, device_id=friend, device_id_type=MESH)

    e_row = lax.broadcasted_iota(jnp.int32, (SIDE * SIDE * CORES, tokens), 0)
    before = (lax.broadcasted_iota(jnp.int32, (tokens, tokens), 0)
              < lax.broadcasted_iota(jnp.int32, (tokens, tokens), 1)).astype(F32).astype(BF)
    for d in range(2):
        ids = ids_ref[d]
        top = ids.shape[0]
        named = jnp.zeros(e_row.shape, F32)
        for j in range(top):
            named += jnp.where(e_row == ids[j:j + 1, :], 1.0, 0.0)
        earlier = jnp.dot(named.astype(BF), before, preferred_element_type=F32)
        spots = [jnp.sum(jnp.where(e_row == ids[j:j + 1, :], earlier, 0.0), axis=0, keepdims=True)
                 for j in range(top)]
        into = tab.at[0] if d == 0 else own_tab
        into[0] = ids.astype(F32) * cap + jnp.concatenate(spots, axis=0)
        into[1] = gate_ref[d].astype(F32) / 64.0

    pl.semaphore_wait(barrier, len(friends))

    def first_hop(sources, dest, own, sib, sem, send_sem):
        for p, sign in enumerate(SIGNS):
            for h in range(CORES):
                for n in (1, 3):
                    da, db = sign * INNER[n][0], sign * INNER[n][1]
                    dev = at(wrap(z + da), wrap(y + db), 0) if h == 0 else at(wrap(z + db), wrap(y + da), 1)
                    send(sources(h, p), dest.at[p, n, c], send_sem, sem, dev)
            send(sources(1 - c, p), dest.at[p, 0, c], send_sem, sib, sibling)
            pltpu.make_async_copy(sources(c, p), dest.at[p, 0, c], own).start()

    def next_hop(dest, sem, send_sem, pairs):
        for p, sign in enumerate(SIGNS):
            for n, m in pairs:
                da, db = (sign * (INNER[m][i] - INNER[n][i]) for i in range(2))
                send(dest.at[p, n], dest.at[p, m], send_sem, sem,
                     at_ab(wrap(mine_a + da), wrap(mine_b + db), c))

    def tables_out(d):
        first_hop(lambda h, p: tab.at[d], tabs.at[d], tab_own_sem.at[d], tab_sib_sem.at[d],
                  tab_hop_sem.at[d, 0], tab_hop_send.at[d, 0])

    def rows_out(s, source, k):
        def part(h, p):
            return source.at[:, pl.ds(pl.multiple_of(h * half + k * WIDE + p * LANES, LANES), LANES)]
        first_hop(part, full.at[s], own_sem.at[s], sib_sem.at[s], hop_sem.at[s, 0], hop_send.at[s, 0])

    def stage_a(s):
        k = s - chunks

        @pl.when(k < 0)
        def _():
            rows_out(s, tok_ref.at[0], s)

        @pl.when(k == 0)
        def _():
            await_bytes(tab.at[1], xt_sem)
            tables_out(1)

        @pl.when(k >= 0)
        def _():
            await_bytes(src.at[:, pl.ds(0, 2 * WIDE)], x_sem.at[k])
            rows_out(s, src, k)

    def stage_b(s):
        d, k = s // chunks, lax.rem(s, chunks)

        @pl.when(k == 0)
        def _():
            await_bytes(tabs.at[d, 0, pl.ds(0, 4)], tab_hop_sem.at[d, 0])
            next_hop(tabs.at[d], tab_hop_sem.at[d, 1], tab_hop_send.at[d, 1], ((1, 2), (3, 4)))

        await_bytes(full.at[s, 0, pl.ds(0, 4)], hop_sem.at[s, 0])
        next_hop(full.at[s], hop_sem.at[s, 1], hop_send.at[s, 1], ((1, 2), (3, 4)))

    def stage_c(s):
        d, k = s // chunks, lax.rem(s, chunks)

        @pl.when(k == 0)
        def _():
            await_bytes(tabs.at[d, 0, pl.ds(0, 4)], tab_hop_sem.at[d, 1])
            next_hop(tabs.at[d], tab_hop_sem.at[d, 2], tab_hop_send.at[d, 2], ((4, 5),))

        await_bytes(full.at[s, 0, pl.ds(0, 4)], hop_sem.at[s, 1])
        next_hop(full.at[s], hop_sem.at[s, 2], hop_send.at[s, 2], ((4, 5),))

    row = lax.broadcasted_iota(jnp.int32, (both, CORES * tokens), 0)
    lane = lax.broadcasted_iota(jnp.int32, (both, CORES * tokens), 1)
    target = jnp.where((row < cap) == (lane < tokens), jnp.where(row < cap, row, row - cap), -2).astype(F32)

    def select_rows(d, p, n, e):
        found = []
        for core in range(CORES):
            t = tabs.at[d, p, n, core]
            local = t[0] - (e * cap).astype(F32)
            hit = (local >= 0.0) & (local < cap)
            spot = jnp.sum(jnp.where(hit, local + 1.0, 0.0), axis=0, keepdims=True) - 1.0
            weight = jnp.sum(jnp.where(hit, t[1], 0.0), axis=0, keepdims=True)
            found.append((spot, weight))
        spot = jnp.concatenate([f[0] for f in found], axis=1)
        weight = jnp.concatenate([f[1] for f in found], axis=1)
        return jnp.where(spot == target, weight, 0.0).astype(BF)

    blocks, start = [], {}
    for p, sign in enumerate(SIGNS):
        for n in range(len(INNER)):
            start[(p, n)] = len(blocks)
            blocks += [(p, n, mine_a, mine_b, c), (p, n, mine_a, mine_b, 1 - c)]
            for da, db in LEAVES[n]:
                blocks += [(p, n, wrap(mine_a + sign * da), wrap(mine_b + sign * db), core) for core in range(CORES)]

    def build_select(d):
        for i, (p, n, a_, b_, core) in enumerate(blocks):
            select[i * both:(i + 1) * both, :] = select_rows(d, p, n, expert_ab(a_, b_, core))

    def origin(p, n):
        a_, b_ = (wrap(at_ - SIGNS[p] * off) for at_, off in zip((mine_a, mine_b), INNER[n]))
        return (1 - c) * a_ + c * b_, (1 - c) * b_ + c * a_

    first_leaf = [sum(len(LEAVES[m]) for m in range(n)) for n in range(len(INNER))]

    def stage_d(s):
        d, k = s // chunks, lax.rem(s, chunks)
        track = lax.rem(s, TRACKS)

        @pl.when(k == 0)
        def _():
            await_bytes(tabs.at[d, 0, pl.ds(0, 2)], tab_hop_sem.at[d, 2])
            await_bytes(tabs.at[d, 0, 0], tab_sib_sem.at[d])
            await_bytes(tabs.at[d, 0, 0], tab_own_sem.at[d])
            build_select(d)

        @pl.when(s >= TRACKS)
        def _():
            await_bytes(to_far.at[track], far_send.at[track])
            await_bytes(to_sib.at[track], sib_send.at[track])

        await_bytes(full.at[s, 0, pl.ds(0, 2)], hop_sem.at[s, 2])
        await_bytes(full.at[s, 0, 0], sib_sem.at[s])
        await_bytes(full.at[s, 0, 0], own_sem.at[s])
        for p in range(2):
            for n in range(len(INNER)):
                rows = full[s, p, n].reshape(CORES * tokens, LANES)
                count = 2 + CORES * len(LEAVES[n])
                got = jnp.dot(select[start[(p, n)] * both:(start[(p, n)] + count) * both, :], rows,
                              preferred_element_type=F32).astype(BF)
                z_, y_ = origin(p, n)

                @pl.when(s < steps - 1)
                def _():
                    tiles[s * CORES + c, z_, y_, :, p * LANES:(p + 1) * LANES] = got[:both]

                @pl.when(s == steps - 1)
                def _():
                    last[c, z_, y_, :, p * LANES:(p + 1) * LANES] = got[:both]

                to_sib[track, p, n] = got[both:2 * both]
                for i in range(len(LEAVES[n])):
                    for core in range(CORES):
                        at_ = (2 + CORES * i + core) * both
                        to_far[track, p, first_leaf[n] + i, core] = got[at_:at_ + both]

        def hand_on(into):
            for p, sign in enumerate(SIGNS):
                for n in range(len(INNER)):
                    z_, y_ = origin(p, n)
                    part = into.at[z_, y_, :, pl.ds(p * LANES, LANES)]
                    for i, (da, db) in enumerate(LEAVES[n]):
                        for core in range(CORES):
                            send(to_far.at[track, p, first_leaf[n] + i, core], part, far_send.at[track],
                                 tile_sem.at[s * CORES + c],
                                 at_ab(wrap(mine_a + sign * da), wrap(mine_b + sign * db), core))
                    send(to_sib.at[track, p, n], part, sib_send.at[track], tile_sem.at[s * CORES + c], sibling)

        @pl.when(s < steps - 1)
        def _():
            hand_on(tiles.at[s * CORES + c])

        @pl.when(s == steps - 1)
        def _():
            hand_on(last.at[c])

    def stage_e(s):
        d, k = s // chunks, lax.rem(s, chunks)
        await_bytes(to_far.at[0, 0], tile_sem.at[s * CORES + c])
        await_bytes(tiles.at[0], tile_sem.at[s * CORES + 1 - c])

        @pl.when(s == chunks)
        def _():
            await_bytes(hid_two, xh_sem)

        def add_product(hid, prior):
            @pl.loop(0, CORES)
            def _(h):
                @pl.loop(0, 1)
                def _(f):
                    rows = pl.ds(f * (units // 1), units // 1)
                    got = jnp.dot(hid[rows, :], tiles[s * CORES + h].reshape(slots, WIDE),
                                  preferred_element_type=F32)
                    if prior:
                        got = got + total[k * CORES + h, rows, :].astype(F32)
                    total[k * CORES + h, rows, :] = got.astype(BF)

        @pl.when(d == 0)
        def _():
            add_product(hid_one, False)

        @pl.when((d == 1) & (s < steps - 1))
        def _():
            add_product(hid_two, True)

    def transpose_hidden(d):
        parts = slots // WIDE
        for n in range((1 - d) * parts, (2 - d) * parts):
            load_hidden(n).wait()
            into = hid_out if n < parts else hid_one
            part = n % parts

            @pl.loop(0, units // WIDE)
            def _(f):
                at_f = pl.multiple_of(f * WIDE, WIDE)
                into[pl.ds(at_f, WIDE), part * WIDE:(part + 1) * WIDE] = stage[n % 2, :, pl.ds(at_f, WIDE)].T

            if n + 2 < 2 * parts:
                load_hidden(n + 2).start()

    for s in range(AHEAD):
        rows_out(s, tok_ref.at[0], s)
        if s == 0:
            tables_out(0)
            send(own_tab, tab.at[1], xsend_sem.at[1], xt_sem, mirror)
    for k in range(chunks):
        for h in range(CORES):
            cols = pl.ds(h * half + k * WIDE, WIDE)
            send(tok_ref.at[1, :, cols], src.at[:, cols], xsend_sem.at[0], x_sem.at[k], mirror)
    stage_b(jnp.int32(0))
    transpose_hidden(1)
    send(hid_out, hid_two, xsend_sem.at[2], xh_sem, mirror)
    stage_b(jnp.int32(1))
    stage_c(jnp.int32(0))
    transpose_hidden(0)

    def turn(i, carry):
        for lag, skip, work in LAGS:
            @pl.when((i - lag >= skip) & (i - lag < steps))
            def _():
                (stage_a, stage_b, stage_c, stage_d, stage_e)[work](i - lag)
        return carry

    lax.fori_loop(AHEAD, steps + LAGS[-1][0], turn, 0)

    for track in range(TRACKS):
        await_bytes(to_far.at[track], far_send.at[track])
        await_bytes(to_sib.at[track], sib_send.at[track])
    await_bytes(src, xsend_sem.at[0])
    await_bytes(own_tab, xsend_sem.at[1])
    await_bytes(hid_out, xsend_sem.at[2])

    @pl.loop(0, steps)
    def _(s):
        for hop, count in enumerate((5, 4, 2)):
            await_bytes(full.at[s, 0, pl.ds(0, count)], hop_send.at[s, hop])

    for d in range(2):
        for hop, count in enumerate((5, 4, 2)):
            await_bytes(tabs.at[d, 0, pl.ds(0, count)], tab_hop_send.at[d, hop])


def finish(total, last, hid_two, out_ref, made, sem):
    count, units, wide = total.shape
    slots = hid_two.shape[1]
    chunks = count // CORES
    piece = units // SIDE

    def put(k, h):
        cols = pl.ds(h * chunks * wide + k * wide, wide)
        rows = total.at[k * CORES + h] if k < chunks - 1 else made.at[h]
        return pltpu.make_async_copy(rows, out_ref.at[:, cols], sem.at[k * CORES + h])

    for k in range(chunks - 1):
        for h in range(CORES):
            put(k, h).start()
    for h in range(CORES):
        @pl.loop(0, SIDE)
        def _(f):
            rows = pl.ds(f * piece, piece)
            got = jnp.dot(hid_two[rows, :], last[h].reshape(slots, wide), preferred_element_type=F32)
            made[h, rows, :] = (got + total[count - CORES + h, rows, :].astype(F32)).astype(BF)
        put(chunks - 1, h).start()
    for k in range(chunks):
        for h in range(CORES):
            put(k, h).wait()


def on_device(ranks, grad_rows, expert_ids, gate_buckets, saved_hidden):
    tok, hid = grad_rows[:, 0], saved_hidden[:, 0, 0]
    ids = expert_ids[:, 0].transpose(0, 2, 1)
    gates = gate_buckets[:, 0].transpose(0, 2, 1)
    tokens, width = tok.shape[1:]
    top = ids.shape[1]
    slots, units = hid.shape[1:]
    cap = slots // (SIDE * SIDE * CORES)
    both = CORES * cap
    steps = width // WIDE
    dma = pltpu.SemaphoreType.DMA
    total, last, hid_two = pl.pallas_call(
        functools.partial(kernel, ranks, cap),
        out_shape=[
            pltpu.VMEM((steps, units, WIDE), BF),
            pltpu.VMEM((CORES, SIDE, SIDE, both, WIDE), BF),
            pltpu.VMEM((units, slots), BF),
        ],
        in_specs=[
            pl.BlockSpec(memory_space=pl.ANY),
            pl.BlockSpec(memory_space=pltpu.VMEM),
            pl.BlockSpec(memory_space=pltpu.VMEM),
            pl.BlockSpec(memory_space=pl.ANY),
        ],
        out_specs=[pl.BlockSpec(memory_space=pltpu.VMEM)] * 3,
        scratch_shapes=[
            pltpu.VMEM((tokens, width), BF),
            pltpu.VMEM((steps, 2, len(INNER), CORES, tokens, LANES), BF),
            pltpu.VMEM(((steps - 1) * CORES, SIDE, SIDE, both, WIDE), BF),
            pltpu.VMEM((units, slots), BF),
            pltpu.VMEM((units, slots), BF),
            pltpu.VMEM((2, WIDE, units), BF),
            pltpu.VMEM((64 * both, CORES * tokens), BF),
            pltpu.VMEM((2, top, tokens), F32),
            pltpu.VMEM((2, 2, top, tokens), F32),
            pltpu.VMEM((2, 2, len(INNER), CORES, 2, top, tokens), F32),
            pltpu.VMEM((TRACKS, 2, 10, CORES, both, LANES), BF),
            pltpu.VMEM((TRACKS, 2, len(INNER), both, LANES), BF),
            dma((steps // 2,)), dma, dma, dma((3,)), dma((2,)),
            dma((steps,)), dma((steps,)), dma((steps, 3)), dma((steps, 3)),
            dma((2,)), dma((2,)), dma((2, 3)), dma((2, 3)),
            dma((steps * CORES,)), dma((TRACKS,)), dma((TRACKS,)),
        ],
        compiler_params=pltpu.CompilerParams(
            collective_id=0, has_side_effects=True, vmem_limit_bytes=VLIM),
    )(tok, ids, gates, hid)
    result = pl.pallas_call(
        finish,
        out_shape=jax.ShapeDtypeStruct((units, width), BF),
        in_specs=[pl.BlockSpec(memory_space=pltpu.VMEM)] * 3,
        out_specs=pl.BlockSpec(memory_space=pl.ANY),
        scratch_shapes=[pltpu.VMEM((CORES, units, WIDE), BF), dma((steps,))],
        compiler_params=pltpu.CompilerParams(vmem_limit_bytes=4 * 1024 * 1024),
    )(total, last, hid_two)
    return result[None, None]


def solution(mesh):
    return jax.shard_map(
        functools.partial(on_device, mesh.shape["pipe"]),
        mesh=mesh,
        in_specs=(
            P(None, "pipe", "expert", None),
            P(None, "pipe", "expert", None),
            P(None, "pipe", "expert", None),
            P(None, "pipe", "expert", None, None),
        ),
        out_specs=P("pipe", "expert", None, None),
        check_vma=False,
    )
```

```python
import functools

import jax
import jax.numpy as jnp
from jax import lax
from jax.experimental import pallas as pl
from jax.experimental.pallas import tpu as pltpu
from jax.sharding import PartitionSpec as P

MESH = pl.DeviceIdType.MESH
SIDE = 4
CORES = 2
LANES = 128
WIDE = 2 * LANES
TRACKS = 4
AHEAD = 4
LAGS = ((0, 4, 0), (2, 2, 1), (3, 1, 2), (4, 0, 3), (6, 0, 4))
VLIM = 48 * 1024 * 1024
INNER = ((0, 0), (0, -1), (-1, -1), (1, 0), (1, 1), (2, 1))
LEAVES = (((0, 1), (-1, 0)), ((0, -1), (1, 0)), ((-1, 0), (0, -1)), ((1, 0),), ((0, 1),), ((0, 1), (1, 0)))
SIGNS = (1, -1)
BF = jnp.bfloat16
F32 = jnp.float32


def wrap(i):
    return lax.rem(i + 2 * SIDE, SIDE)


def kernel(ranks, cap, tok_ref, ids_ref, gate_ref, hid_ref, total, last, hid_two,
           src, full, tiles, hid_one, hid_out, stage, select, own_tab, tab, tabs,
           to_far, to_sib,
           x_sem, xt_sem, xh_sem, xsend_sem, stage_sem,
           own_sem, sib_sem, hop_sem, hop_send,
           tab_own_sem, tab_sib_sem, tab_hop_sem, tab_hop_send,
           tile_sem, far_send, sib_send):
    tokens, width = tok_ref.shape[1], tok_ref.shape[2]
    slots, units = hid_ref.shape[1], hid_ref.shape[2]
    half = width // CORES
    chunks = half // WIDE
    steps = 2 * chunks
    both = CORES * cap

    rank = lax.axis_index("pipe")
    expert = lax.axis_index("expert")
    c = lax.rem(expert, CORES)
    y = lax.rem(expert // CORES, SIDE)
    z = expert // (CORES * SIDE)
    mine_a = (1 - c) * z + c * y
    mine_b = (1 - c) * y + c * z
    def at(z_, y_, core):
        return {"pipe": rank, "expert": (z_ * SIDE + y_) * CORES + core}

    def at_ab(a_, b_, core):
        return at((1 - c) * a_ + c * b_, (1 - c) * b_ + c * a_, core)

    def expert_ab(a_, b_, core):
        return (((1 - c) * a_ + c * b_) * SIDE + (1 - c) * b_ + c * a_) * CORES + core

    sibling = at(z, y, 1 - c)
    mirror = {"pipe": ranks - 1 - rank, "expert": expert}

    def send(s_ref, d_ref, s_sem, r_sem, dev):
        pltpu.make_async_remote_copy(
            src_ref=s_ref, dst_ref=d_ref, send_sem=s_sem, recv_sem=r_sem,
            device_id=dev, device_id_type=MESH).start()

    def await_bytes(ref, sem):
        pltpu.make_async_copy(ref, ref, sem).wait()

    def load_hidden(n):
        d, part = (1, n) if n < slots // WIDE else (0, n - slots // WIDE)
        return pltpu.make_async_copy(
            hid_ref.at[d, pl.ds(part * WIDE, WIDE)], stage.at[n % 2], stage_sem.at[n % 2])

    load_hidden(0).start()
    load_hidden(1).start()

    barrier = pltpu.get_barrier_semaphore()
    friends = [sibling, mirror]
    for core in range(CORES):
        for turn in (1, SIDE - 1):
            friends.append(at(wrap(z + turn), y, core))
            friends.append(at(z, wrap(y + turn), core))
    for friend in friends:
        pl.semaphore_signal(barrier, inc=1, device_id=friend, device_id_type=MESH)

    e_row = lax.broadcasted_iota(jnp.int32, (SIDE * SIDE * CORES, tokens), 0)
    before = (lax.broadcasted_iota(jnp.int32, (tokens, tokens), 0)
              < lax.broadcasted_iota(jnp.int32, (tokens, tokens), 1)).astype(F32).astype(BF)
    for d in range(2):
        ids = ids_ref[d]
        top = ids.shape[0]
        named = jnp.zeros(e_row.shape, F32)
        for j in range(top):
            named += jnp.where(e_row == ids[j:j + 1, :], 1.0, 0.0)
        earlier = jnp.dot(named.astype(BF), before, preferred_element_type=F32)
        spots = [jnp.sum(jnp.where(e_row == ids[j:j + 1, :], earlier, 0.0), axis=0, keepdims=True)
                 for j in range(top)]
        into = tab.at[0] if d == 0 else own_tab
        into[0] = ids.astype(F32) * cap + jnp.concatenate(spots, axis=0)
        into[1] = gate_ref[d].astype(F32) / 64.0

    pl.semaphore_wait(barrier, len(friends))

    def first_hop(sources, dest, own, sib, sem, send_sem):
        for p, sign in enumerate(SIGNS):
            for h in range(CORES):
                for n in (1, 3):
                    da, db = sign * INNER[n][0], sign * INNER[n][1]
                    dev = at(wrap(z + da), wrap(y + db), 0) if h == 0 else at(wrap(z + db), wrap(y + da), 1)
                    send(sources(h, p), dest.at[p, n, c], send_sem, sem, dev)
            send(sources(1 - c, p), dest.at[p, 0, c], send_sem, sib, sibling)
            pltpu.make_async_copy(sources(c, p), dest.at[p, 0, c], own).start()

    def next_hop(dest, sem, send_sem, pairs):
        for p, sign in enumerate(SIGNS):
            for n, m in pairs:
                da, db = (sign * (INNER[m][i] - INNER[n][i]) for i in range(2))
                send(dest.at[p, n], dest.at[p, m], send_sem, sem,
                     at_ab(wrap(mine_a + da), wrap(mine_b + db), c))

    def tables_out(d):
        first_hop(lambda h, p: tab.at[d], tabs.at[d], tab_own_sem.at[d], tab_sib_sem.at[d],
                  tab_hop_sem.at[d, 0], tab_hop_send.at[d, 0])

    def rows_out(s, source, k):
        def part(h, p):
            return source.at[:, pl.ds(pl.multiple_of(h * half + k * WIDE + p * LANES, LANES), LANES)]
        first_hop(part, full.at[s], own_sem.at[s], sib_sem.at[s], hop_sem.at[s, 0], hop_send.at[s, 0])

    def stage_a(s):
        k = s - chunks

        @pl.when(k < 0)
        def _():
            rows_out(s, tok_ref.at[0], s)

        @pl.when(k == 0)
        def _():
            await_bytes(tab.at[1], xt_sem)
            tables_out(1)

        @pl.when(k >= 0)
        def _():
            await_bytes(src.at[:, pl.ds(0, 2 * WIDE)], x_sem.at[k])
            rows_out(s, src, k)

    def stage_b(s):
        d, k = s // chunks, lax.rem(s, chunks)

        @pl.when(k == 0)
        def _():
            await_bytes(tabs.at[d, 0, pl.ds(0, 4)], tab_hop_sem.at[d, 0])
            next_hop(tabs.at[d], tab_hop_sem.at[d, 1], tab_hop_send.at[d, 1], ((1, 2), (3, 4)))

        await_bytes(full.at[s, 0, pl.ds(0, 4)], hop_sem.at[s, 0])
        next_hop(full.at[s], hop_sem.at[s, 1], hop_send.at[s, 1], ((1, 2), (3, 4)))

    def stage_c(s):
        d, k = s // chunks, lax.rem(s, chunks)

        @pl.when(k == 0)
        def _():
            await_bytes(tabs.at[d, 0, pl.ds(0, 4)], tab_hop_sem.at[d, 1])
            next_hop(tabs.at[d], tab_hop_sem.at[d, 2], tab_hop_send.at[d, 2], ((4, 5),))

        await_bytes(full.at[s, 0, pl.ds(0, 4)], hop_sem.at[s, 1])
        next_hop(full.at[s], hop_sem.at[s, 2], hop_send.at[s, 2], ((4, 5),))

    row = lax.broadcasted_iota(jnp.int32, (both, CORES * tokens), 0)
    lane = lax.broadcasted_iota(jnp.int32, (both, CORES * tokens), 1)
    target = jnp.where((row < cap) == (lane < tokens), jnp.where(row < cap, row, row - cap), -2).astype(F32)

    def select_rows(d, p, n, e):
        found = []
        for core in range(CORES):
            t = tabs.at[d, p, n, core]
            local = t[0] - (e * cap).astype(F32)
            hit = (local >= 0.0) & (local < cap)
            spot = jnp.sum(jnp.where(hit, local + 1.0, 0.0), axis=0, keepdims=True) - 1.0
            weight = jnp.sum(jnp.where(hit, t[1], 0.0), axis=0, keepdims=True)
            found.append((spot, weight))
        spot = jnp.concatenate([f[0] for f in found], axis=1)
        weight = jnp.concatenate([f[1] for f in found], axis=1)
        return jnp.where(spot == target, weight, 0.0).astype(BF)

    blocks, start = [], {}
    for p, sign in enumerate(SIGNS):
        for n in range(len(INNER)):
            start[(p, n)] = len(blocks)
            blocks += [(p, n, mine_a, mine_b, c), (p, n, mine_a, mine_b, 1 - c)]
            for da, db in LEAVES[n]:
                blocks += [(p, n, wrap(mine_a + sign * da), wrap(mine_b + sign * db), core) for core in range(CORES)]

    def build_select(d):
        for i, (p, n, a_, b_, core) in enumerate(blocks):
            select[i * both:(i + 1) * both, :] = select_rows(d, p, n, expert_ab(a_, b_, core))

    def origin(p, n):
        a_, b_ = (wrap(at_ - SIGNS[p] * off) for at_, off in zip((mine_a, mine_b), INNER[n]))
        return (1 - c) * a_ + c * b_, (1 - c) * b_ + c * a_

    first_leaf = [sum(len(LEAVES[m]) for m in range(n)) for n in range(len(INNER))]

    def stage_d(s):
        d, k = s // chunks, lax.rem(s, chunks)
        track = lax.rem(s, TRACKS)

        @pl.when(k == 0)
        def _():
            await_bytes(tabs.at[d, 0, pl.ds(0, 2)], tab_hop_sem.at[d, 2])
            await_bytes(tabs.at[d, 0, 0], tab_sib_sem.at[d])
            await_bytes(tabs.at[d, 0, 0], tab_own_sem.at[d])
            build_select(d)

        @pl.when(s >= TRACKS)
        def _():
            await_bytes(to_far.at[track], far_send.at[track])
            await_bytes(to_sib.at[track], sib_send.at[track])

        await_bytes(full.at[s, 0, pl.ds(0, 2)], hop_sem.at[s, 2])
        await_bytes(full.at[s, 0, 0], sib_sem.at[s])
        await_bytes(full.at[s, 0, 0], own_sem.at[s])
        def place(p):
            for n in range(len(INNER)):
                rows = full[s, p, n].reshape(CORES * tokens, LANES)
                count = 2 + CORES * len(LEAVES[n])
                got = jnp.dot(select[start[(p, n)] * both:(start[(p, n)] + count) * both, :], rows,
                              preferred_element_type=F32).astype(BF)
                z_, y_ = origin(p, n)

                tiles[lax.rem(s, steps - 1) * CORES + c, z_, y_, :, p * LANES:(p + 1) * LANES] = got[:both]
                last[c, z_, y_, :, p * LANES:(p + 1) * LANES] = got[:both]
                to_sib[track, p, n] = got[both:2 * both]
                for i in range(len(LEAVES[n])):
                    for core in range(CORES):
                        at_ = (2 + CORES * i + core) * both
                        to_far[track, p, first_leaf[n] + i, core] = got[at_:at_ + both]

        def hand_on(into, p):
            sign = SIGNS[p]
            for n in range(len(INNER)):
                z_, y_ = origin(p, n)
                part = into.at[z_, y_, :, pl.ds(p * LANES, LANES)]
                for i, (da, db) in enumerate(LEAVES[n]):
                    for core in range(CORES):
                        send(to_far.at[track, p, first_leaf[n] + i, core], part, far_send.at[track],
                             tile_sem.at[s * CORES + c],
                             at_ab(wrap(mine_a + sign * da), wrap(mine_b + sign * db), core))
                send(to_sib.at[track, p, n], part, sib_send.at[track], tile_sem.at[s * CORES + c], sibling)

        for p in range(2):
            place(p)

            @pl.when(s < steps - 1)
            def _():
                hand_on(tiles.at[s * CORES + c], p)

            @pl.when(s == steps - 1)
            def _():
                hand_on(last.at[c], p)

    def stage_e(s):
        d, k = s // chunks, lax.rem(s, chunks)
        await_bytes(to_far.at[0, 0], tile_sem.at[s * CORES + c])
        await_bytes(tiles.at[0], tile_sem.at[s * CORES + 1 - c])

        @pl.when(s == chunks)
        def _():
            await_bytes(hid_two, xh_sem)

        def add_product(hid, prior):
            for h in range(CORES):
                got = jnp.dot(hid[...], tiles[s * CORES + h].reshape(slots, WIDE), preferred_element_type=F32)
                if prior:
                    got = got + total[k * CORES + h].astype(F32)
                total[k * CORES + h] = got.astype(BF)

        @pl.when(d == 0)
        def _():
            add_product(hid_one, False)

        @pl.when((d == 1) & (s < steps - 1))
        def _():
            add_product(hid_two, True)

    def transpose_hidden(d):
        parts = slots // WIDE
        for n in range((1 - d) * parts, (2 - d) * parts):
            load_hidden(n).wait()
            into = hid_out if n < parts else hid_one
            part = n % parts

            @pl.loop(0, units // WIDE)
            def _(f):
                at_f = pl.multiple_of(f * WIDE, WIDE)
                into[pl.ds(at_f, WIDE), part * WIDE:(part + 1) * WIDE] = stage[n % 2, :, pl.ds(at_f, WIDE)].T

            if n + 2 < 2 * parts:
                load_hidden(n + 2).start()

    for s in range(AHEAD):
        rows_out(s, tok_ref.at[0], s)
        if s == 0:
            tables_out(0)
            send(own_tab, tab.at[1], xsend_sem.at[1], xt_sem, mirror)
    for k in range(chunks):
        for h in range(CORES):
            cols = pl.ds(h * half + k * WIDE, WIDE)
            send(tok_ref.at[1, :, cols], src.at[:, cols], xsend_sem.at[0], x_sem.at[k], mirror)
    stage_b(jnp.int32(0))
    transpose_hidden(1)
    send(hid_out, hid_two, xsend_sem.at[2], xh_sem, mirror)
    stage_b(jnp.int32(1))
    stage_c(jnp.int32(0))
    transpose_hidden(0)

    def turn(i, carry):
        for lag, skip, work in LAGS:
            @pl.when((i - lag >= skip) & (i - lag < steps))
            def _():
                (stage_a, stage_b, stage_c, stage_d, stage_e)[work](i - lag)
        return carry

    lax.fori_loop(AHEAD, steps + max(lag for lag, _, _ in LAGS), turn, 0)

    for track in range(TRACKS):
        await_bytes(to_far.at[track], far_send.at[track])
        await_bytes(to_sib.at[track], sib_send.at[track])
    await_bytes(src, xsend_sem.at[0])
    await_bytes(own_tab, xsend_sem.at[1])
    await_bytes(hid_out, xsend_sem.at[2])

    @pl.loop(0, steps)
    def _(s):
        for hop, count in enumerate((5, 4, 2)):
            await_bytes(full.at[s, 0, pl.ds(0, count)], hop_send.at[s, hop])

    for d in range(2):
        for hop, count in enumerate((5, 4, 2)):
            await_bytes(tabs.at[d, 0, pl.ds(0, count)], tab_hop_send.at[d, hop])


def finish(total, last, hid_two, out_ref, made, sem):
    count, units, wide = total.shape
    slots = hid_two.shape[1]
    chunks = count // CORES

    def put(k, h):
        cols = pl.ds(h * chunks * wide + k * wide, wide)
        rows = total.at[k * CORES + h] if k < chunks - 1 else made.at[h]
        return pltpu.make_async_copy(rows, out_ref.at[:, cols], sem.at[k * CORES + h])

    for k in range(chunks - 1):
        for h in range(CORES):
            put(k, h).start()
    for h in range(CORES):
        @pl.loop(0, SIDE)
        def _(f):
            rows = pl.ds(f * (units // SIDE), units // SIDE)
            got = jnp.dot(hid_two[rows, :], last[h].reshape(slots, wide), preferred_element_type=F32)
            made[h, rows, :] = (got + total[count - CORES + h, rows, :].astype(F32)).astype(BF)

        put(chunks - 1, h).start()
    for k in range(chunks):
        for h in range(CORES):
            put(k, h).wait()


def on_device(ranks, grad_rows, expert_ids, gate_buckets, saved_hidden):
    tok, hid = grad_rows[:, 0], saved_hidden[:, 0, 0]
    ids = expert_ids[:, 0].transpose(0, 2, 1)
    gates = gate_buckets[:, 0].transpose(0, 2, 1)
    tokens, width = tok.shape[1:]
    top = ids.shape[1]
    slots, units = hid.shape[1:]
    cap = slots // (SIDE * SIDE * CORES)
    both = CORES * cap
    steps = width // WIDE
    dma = pltpu.SemaphoreType.DMA
    total, last, hid_two = pl.pallas_call(
        functools.partial(kernel, ranks, cap),
        out_shape=[
            pltpu.VMEM((steps, units, WIDE), BF),
            pltpu.VMEM((CORES, SIDE, SIDE, both, WIDE), BF),
            pltpu.VMEM((units, slots), BF),
        ],
        in_specs=[
            pl.BlockSpec(memory_space=pl.ANY),
            pl.BlockSpec(memory_space=pltpu.VMEM),
            pl.BlockSpec(memory_space=pltpu.VMEM),
            pl.BlockSpec(memory_space=pl.ANY),
        ],
        out_specs=[pl.BlockSpec(memory_space=pltpu.VMEM)] * 3,
        scratch_shapes=[
            pltpu.VMEM((tokens, width), BF),
            pltpu.VMEM((steps, 2, len(INNER), CORES, tokens, LANES), BF),
            pltpu.VMEM(((steps - 1) * CORES, SIDE, SIDE, both, WIDE), BF),
            pltpu.VMEM((units, slots), BF),
            pltpu.VMEM((units, slots), BF),
            pltpu.VMEM((2, WIDE, units), BF),
            pltpu.VMEM((64 * both, CORES * tokens), BF),
            pltpu.VMEM((2, top, tokens), F32),
            pltpu.VMEM((2, 2, top, tokens), F32),
            pltpu.VMEM((2, 2, len(INNER), CORES, 2, top, tokens), F32),
            pltpu.VMEM((TRACKS, 2, 10, CORES, both, LANES), BF),
            pltpu.VMEM((TRACKS, 2, len(INNER), both, LANES), BF),
            dma((steps // 2,)), dma, dma, dma((3,)), dma((2,)),
            dma((steps,)), dma((steps,)), dma((steps, 3)), dma((steps, 3)),
            dma((2,)), dma((2,)), dma((2, 3)), dma((2, 3)),
            dma((steps * CORES,)), dma((TRACKS,)), dma((TRACKS,)),
        ],
        compiler_params=pltpu.CompilerParams(
            collective_id=0, has_side_effects=True, vmem_limit_bytes=VLIM),
    )(tok, ids, gates, hid)
    result = pl.pallas_call(
        finish,
        out_shape=jax.ShapeDtypeStruct((units, width), BF),
        in_specs=[pl.BlockSpec(memory_space=pltpu.VMEM)] * 3,
        out_specs=pl.BlockSpec(memory_space=pl.ANY),
        scratch_shapes=[pltpu.VMEM((CORES, units, WIDE), BF), dma((steps,))],
        compiler_params=pltpu.CompilerParams(vmem_limit_bytes=4 * 1024 * 1024),
    )(total, last, hid_two)
    return result[None, None]


def solution(mesh):
    return jax.shard_map(
        functools.partial(on_device, mesh.shape["pipe"]),
        mesh=mesh,
        in_specs=(
            P(None, "pipe", "expert", None),
            P(None, "pipe", "expert", None),
            P(None, "pipe", "expert", None),
            P(None, "pipe", "expert", None, None),
        ),
        out_specs=P("pipe", "expert", None, None),
        check_vma=False,
    )
```
